512 devices in a mesh: row: 128 (over y, z, core), col: 4 (over x).
Axes of the slice: x: 4, y: 8, z: 8, core: 2. Of those that a mesh axis runs over, the one named last changes fastest.
Arguments:
- hidden: bfloat16 [65536, 1152], P('row', 'col'), may hold values from -60 to 60
- noisy_latent: bfloat16 [8192, 128], P('row'), may hold values from -6 to 6
- tile_latent: int32 [512], replicated, may hold values from 0 to 254, as said below
- timesteps: int32 [512], replicated, may hold values from 0 to 49
- step_embedding: bfloat16 [50, 1152], replicated, may hold values from -6 to 6
- alpha_now: float32 [50], replicated, may hold values from 0.25 to 0.95
- alpha_next: float32 [50], replicated, may hold values from 0.3 to 0.99
- modulation: bfloat16 [1152, 8, 1152], P('row', None, 'col'), may hold values from -0.1875 to 0.1875
- attention_in: bfloat16 [1152, 3, 1152], P(None, None, 'col'), may hold values from -6 to 6
- attention_out: bfloat16 [1152, 1152], P('col'), may hold values from -0.1875 to 0.1875
- expand_weight: bfloat16 [1152, 2304], P('row', 'col'), may hold values from -0.1875 to 0.1875
- reduce_weight: bfloat16 [2304, 1152], P('col', 'row'), may hold values from -0.125 to 0.125
- noise_head: bfloat16 [1152, 16], P('col'), may hold values from -0.1875 to 0.1875
- preview_kernel: float32 [3, 3, 4, 4], replicated, may hold values from -1 to 1
Outputs:
- stepped: bfloat16 [8192, 128], P('row')
- preview: bfloat16 [8192, 128], P('row')
The draws below stay inside these ranges and needn't reach their ends.
Inputs may be any that keep to these rules, and one draw needn't show every extreme that they name: `tile_latent`: latent ids start at 0 on the first tile and rise by 0 or 1 from one tile to the next; the first 4 tiles form latent 0, and every later aligned group of 4 tiles holds exactly two latents of 1 to 3 consecutive tiles each.
All inputs are finite; a program needn't handle non-finite values.
Results may differ from the reference program's by a relative error of at most 0.015.
Values may be sent and summed in bfloat16 or wider, within the bound.
A program may use at most 64 MiB of HBM per device.

```python
import jax
import jax.numpy as jnp
from jax import lax

D = 1152
HEADS = 16
HEAD_DIM = 72
PATCH = 2
CHANNELS = 4
FF = 2304
GRIDW = 16
TILE_ROWS = 8
MAXT = 4
STEPS = 50
TILE = 128
TILES_ALL = 512
TOKENS = 65536
NLAT = 512
LROWS = 8192
LWIDTH = 128
NOISE = 16
N_COL = 4


def draw_hidden(key, part):
    base_key = jax.random.fold_in(jax.random.fold_in(key, 11), 0)
    base_rows = jnp.clip(jax.random.normal(base_key, (TOKENS, D), jnp.float32), -6.0, 6.0)
    return base_rows.astype(jnp.bfloat16)


def draw_attention_in(key, part):
    base_key = jax.random.fold_in(jax.random.fold_in(key, 23), 0)
    weights = jnp.clip(jax.random.normal(base_key, (D, 3, D), jnp.float32), -6.0, 6.0) * D ** (-0.5)
    return jnp.clip(weights, -6.0, 6.0).astype(jnp.bfloat16)


def draw_tile_latent(key, part):
    split_key = jax.random.fold_in(key, 37)
    groups = TILES_ALL // MAXT
    index = jnp.arange(TILES_ALL, dtype=jnp.int32)
    split_at = jax.random.randint(split_key, (groups,), 1, MAXT, jnp.int32)
    within = index % MAXT
    group_of = index // MAXT
    split_here = jnp.repeat(split_at, MAXT)
    breaks = jnp.where((within == 0) | (within == split_here), 1, 0)
    breaks = jnp.where(group_of == 0, 0, breaks)
    return jnp.cumsum(breaks).astype(jnp.int32)


def with_ends(result, own_key, smallest, largest):
    place = [jax.random.randint(jax.random.fold_in(own_key, axis), (), 0, length) for axis, length in enumerate(result.shape)]
    main_axis = result.shape.index(max(result.shape))
    neighbour = place[:main_axis] + [(place[main_axis] + 1) % result.shape[main_axis]] + place[main_axis + 1:]
    return result.at[tuple(place)].set(smallest).at[tuple(neighbour)].set(largest)


def levels(key, dims, cuts, least, top_value):
    factor_of, own = 1.0, jax.random.fold_in(key, 6)
    for dim, parts in cuts:
        heights = jnp.exp(jax.random.uniform(jax.random.fold_in(own, dim), (parts,), jnp.float32, least / len(cuts), top_value / len(cuts)))
        factor_of = factor_of * jnp.repeat(heights, dims[dim] // parts).reshape([-1 if axis == dim else 1 for axis in range(len(dims))])
    return factor_of


def bell_draw(rng, extent, deviation, reach, cuts=(), held_as=jnp.bfloat16):
    array = deviation * jax.random.normal(rng, extent, jnp.float32)
    if cuts:
        array = array * levels(rng, extent, cuts, -0.22, 0.18)
    return jnp.clip(array, -reach, reach).astype(held_as)


def setup_inputs(seed: int = 0) -> dict:
    key_of = jax.random.split(jax.random.key(seed), 15)
    hidden = draw_hidden(jax.random.fold_in(key_of[14], 71), 0)
    noisy_latent = bell_draw(key_of[1], (LROWS, LWIDTH), 1.0, 6.0, ((0, 128),))
    tile_latent = draw_tile_latent(jax.random.fold_in(key_of[14], 71), 0)
    timesteps = with_ends(jax.random.randint(key_of[3], (NLAT,), 0, STEPS), jax.random.fold_in(key_of[3], 1), 0, STEPS - 1).astype(jnp.int32)
    step_embedding = bell_draw(key_of[4], (STEPS, D), 1.0, 6.0)
    alpha_now = jnp.clip(jax.random.uniform(key_of[5], (STEPS,), jnp.float32, 0.25, 0.95), 0.25, 0.95)
    alpha_next = jnp.clip(jax.random.uniform(key_of[6], (STEPS,), jnp.float32, 0.3, 0.99), 0.3, 0.99)
    modulation = bell_draw(key_of[7], (D, 8, D), D ** -0.5, 0.1875, ((0, 128), (2, 4)))
    attention_in = draw_attention_in(jax.random.fold_in(key_of[14], 71), 0)
    attention_out = bell_draw(key_of[9], (D, D), D ** -0.5, 0.1875, ((0, 4),))
    expand_weight = bell_draw(key_of[10], (D, FF), D ** -0.5, 0.1875, ((0, 128), (1, 4)))
    reduce_weight = bell_draw(key_of[11], (FF, D), FF ** -0.5, 0.125, ((0, 4), (1, 128)))
    noise_head = bell_draw(key_of[12], (D, NOISE), D ** -0.5, 0.1875, ((0, 4),))
    preview_kernel = bell_draw(key_of[13], (3, 3, CHANNELS, CHANNELS), (9 * CHANNELS) ** -0.5, 1.0, (), jnp.float32)
    return {"hidden": hidden, "noisy_latent": noisy_latent, "tile_latent": tile_latent, "timesteps": timesteps, "step_embedding": step_embedding, "alpha_now": alpha_now, "alpha_next": alpha_next, "modulation": modulation, "attention_in": attention_in, "attention_out": attention_out, "expand_weight": expand_weight, "reduce_weight": reduce_weight, "noise_head": noise_head, "preview_kernel": preview_kernel}


EPS_NORM = 1e-06

def modulate_tiles(values, shift_term, scale_term):
    mean_value = lax.optimization_barrier(jnp.sum(values, axis=-1, keepdims=True)) / D
    spread = lax.optimization_barrier(jnp.sum(values * values, axis=-1, keepdims=True)) / D - mean_value * mean_value
    normed = (values - mean_value) * lax.rsqrt(spread + EPS_NORM)
    return normed * (1.0 + scale_term[:, None, :]) + shift_term[:, None, :]

def round_trip(values):
    return lax.optimization_barrier(values.astype(jnp.bfloat16)).astype(jnp.float32)

def conv_bands(kernel):
    pixels = GRIDW * PATCH
    in_pixel = jnp.arange(pixels)[:, None]
    out_pixel = jnp.arange(pixels)[None, :]
    band_list = []
    for row_off in range(3):
        summed = jnp.zeros((pixels, CHANNELS, pixels, CHANNELS), jnp.float32)
        for col_off in range(3):
            shifted = (in_pixel == out_pixel + col_off - 1).astype(jnp.float32)
            summed = summed + shifted[:, None, :, None] * kernel[row_off, col_off][None, :, None, :]
        band_list.append(summed.reshape(pixels * CHANNELS, pixels * CHANNELS))
    return band_list

def reference(hidden, noisy_latent, tile_latent, timesteps, step_embedding, alpha_now, alpha_next, modulation, attention_in, attention_out, expand_weight, reduce_weight, noise_head, preview_kernel):
    tiles_all = tile_latent.shape[0]
    tile_steps = timesteps[tile_latent]
    conditioning = jax.nn.silu(step_embedding[tile_steps].astype(jnp.float32)).astype(jnp.bfloat16)
    adaptive = jnp.dot(conditioning, modulation.reshape(D, 8 * D), preferred_element_type=jnp.float32).reshape(tiles_all, 8, D)
    group_tiles = 32
    group_count = tiles_all // group_tiles
    tokens_grouped = hidden.reshape(group_count, group_tiles, TILE, D)
    adaptive_grouped = adaptive.reshape(group_count, group_tiles, 8, D)

    def attention_inputs(packed):
        tokens, rows_adapt = packed
        normed = modulate_tiles(tokens.astype(jnp.float32), rows_adapt[:, 0], rows_adapt[:, 1]).astype(jnp.bfloat16)
        triple = jnp.dot(normed.reshape(-1, D), attention_in.reshape(D, 3 * D), preferred_element_type=jnp.float32)
        return triple.astype(jnp.bfloat16).reshape(group_tiles, TILE, 3, D)
    triple = lax.map(attention_inputs, (tokens_grouped, adaptive_grouped)).reshape(tiles_all, TILE, 3, D)
    reach_tiles = MAXT - 1
    window = 2 * reach_tiles + 1
    pad_ids = jnp.full((reach_tiles,), -1, jnp.int32)
    padded_ids = jnp.concatenate([pad_ids, tile_latent.astype(jnp.int32), pad_ids])
    key_pairs = jnp.pad(triple[:, :, 1:], ((reach_tiles, reach_tiles), (0, 0), (0, 0), (0, 0)))
    scale_factor = HEAD_DIM ** (-0.5)

    def attend_tile(tile_index):
        queries = triple[tile_index, :, 0].reshape(TILE, HEADS, HEAD_DIM).astype(jnp.float32)
        nearby = lax.dynamic_slice_in_dim(key_pairs, tile_index, window, 0)
        nearby = nearby.reshape(window * TILE, 2, HEADS, HEAD_DIM).astype(jnp.float32)
        window_ids = lax.dynamic_slice_in_dim(padded_ids, tile_index, window, 0)
        allowed = jnp.repeat(window_ids == tile_latent[tile_index], TILE)
        scores = jnp.einsum('qhd,khd->hqk', queries, nearby[:, 0]) * scale_factor
        scores = jnp.where(allowed[None, None, :], scores, -1e+30)
        row_peak = lax.optimization_barrier(jnp.max(scores, axis=2, keepdims=True))
        raised = jnp.exp(scores - row_peak)
        weights = round_trip(raised / lax.optimization_barrier(jnp.sum(raised, axis=2, keepdims=True)))
        mixed = jnp.einsum('hqk,khd->qhd', weights, nearby[:, 1])
        return mixed.reshape(TILE, D).astype(jnp.bfloat16)
    attended = lax.map(attend_tile, jnp.arange(tiles_all, dtype=jnp.int32))
    attended_grouped = attended.reshape(group_count, group_tiles, TILE, D)
    cols_block = D // N_COL
    units_block = FF // N_COL

    def block_rest(packed):
        tokens, attended_rows, rows_adapt = packed
        flat_rows = attended_rows.reshape(-1, D)
        attn_sum = jnp.zeros((group_tiles * TILE, D), jnp.float32)
        for block_index in range(N_COL):
            part_rows = flat_rows[:, block_index * cols_block:(block_index + 1) * cols_block]
            part_weight = attention_out[block_index * cols_block:(block_index + 1) * cols_block]
            attn_sum = attn_sum + round_trip(jnp.dot(part_rows, part_weight, preferred_element_type=jnp.float32))
        residual = (tokens.astype(jnp.float32) + rows_adapt[:, 2][:, None, :] * attn_sum.reshape(group_tiles, TILE, D)).astype(jnp.bfloat16)
        normed_mid = modulate_tiles(residual.astype(jnp.float32), rows_adapt[:, 3], rows_adapt[:, 4]).astype(jnp.bfloat16)
        expanded = jnp.dot(normed_mid.reshape(-1, D), expand_weight, preferred_element_type=jnp.float32)
        activated = jax.nn.gelu(expanded, approximate=True).astype(jnp.bfloat16)
        mlp_sum = jnp.zeros((group_tiles * TILE, D), jnp.float32)
        for block_index in range(N_COL):
            part_rows = activated[:, block_index * units_block:(block_index + 1) * units_block]
            part_weight = reduce_weight[block_index * units_block:(block_index + 1) * units_block]
            mlp_sum = mlp_sum + round_trip(jnp.dot(part_rows, part_weight, preferred_element_type=jnp.float32))
        second = (residual.astype(jnp.float32) + rows_adapt[:, 5][:, None, :] * mlp_sum.reshape(group_tiles, TILE, D)).astype(jnp.bfloat16)
        normed_out = modulate_tiles(second.astype(jnp.float32), rows_adapt[:, 6], rows_adapt[:, 7]).astype(jnp.bfloat16)
        return jnp.dot(normed_out.reshape(-1, D), noise_head, preferred_element_type=jnp.float32)
    noise_pred = lax.map(block_rest, (tokens_grouped, attended_grouped, adaptive_grouped))
    noise_img = noise_pred.reshape(tiles_all, TILE_ROWS, GRIDW, PATCH, PATCH, CHANNELS)
    noise_img = noise_img.transpose(0, 1, 3, 2, 4, 5).reshape(LROWS, LWIDTH)
    row_latent = jnp.repeat(tile_latent.astype(jnp.int32), TILE_ROWS * PATCH)
    row_steps = timesteps[row_latent]
    signal_now = alpha_now[row_steps][:, None]
    signal_next = alpha_next[row_steps][:, None]
    noisy_rows = noisy_latent.astype(jnp.float32)
    clean_rows = (noisy_rows - jnp.sqrt(1.0 - signal_now) * noise_img) / jnp.sqrt(signal_now)
    stepped = (jnp.sqrt(signal_next) * clean_rows + jnp.sqrt(1.0 - signal_next) * noise_img).astype(jnp.bfloat16)
    band_list = conv_bands(preview_kernel)
    empty_row = jnp.zeros((1, LWIDTH), jnp.float32)
    above_rows = jnp.concatenate([empty_row, clean_rows[:-1]], axis=0)
    below_rows = jnp.concatenate([clean_rows[1:], empty_row], axis=0)
    edge_id = jnp.full((1,), -1, jnp.int32)
    above_ok = (jnp.concatenate([edge_id, row_latent[:-1]]) == row_latent)[:, None]
    below_ok = (jnp.concatenate([row_latent[1:], edge_id]) == row_latent)[:, None]
    highest = lax.Precision.HIGHEST
    preview = jnp.where(above_ok, jnp.dot(above_rows, band_list[0], precision=highest), 0.0) + jnp.dot(clean_rows, band_list[1], precision=highest) + jnp.where(below_ok, jnp.dot(below_rows, band_list[2], precision=highest), 0.0)
    return (stepped, preview.astype(jnp.bfloat16))
```

```python
import functools

import jax
import jax.numpy as jnp
import numpy as np
from jax import lax
from jax.experimental import pallas as pl
from jax.experimental.pallas import tpu as pltpu
from jax.sharding import PartitionSpec as P

D = 1152
HEAD_DIM = 72
HEADS_HERE = 4
GRIDW = 16
STEPS = 50
TILE = 128
NX, NY, NZ = 4, 8, 8
COLS = D // NX
UNITS = 2304 // NX
ROWS = 9
BLOCK = 144
EPS_NORM = 1e-06
MESH = pl.DeviceIdType.MESH
F32 = jnp.float32
BF16 = jnp.bfloat16
CHUNKS = ((0, 48), (48, 32), (80, 32), (112, 32))


def swapped_order():
    index = np.arange(D)
    major, minor, word = index // 144, (index % 144) // 18, index % 18
    return (minor * 144 + major * 18 + word).astype(np.int32).reshape(D, 1)


def iota(shape, dim):
    return lax.broadcasted_iota(jnp.int32, shape, dim)


def dot(a, b):
    return jnp.dot(a, b, preferred_element_type=F32)


def dot_nt(a, b):
    return lax.dot_general(a, b, (((1,), (1,)), ((), ())), preferred_element_type=F32)


def exact_dot(a, b):
    return jnp.dot(a, b, preferred_element_type=F32, precision=lax.Precision.HIGHEST)


def normalized(values):
    mean_value = jnp.sum(values, axis=1, keepdims=True) / D
    spread = jnp.sum(values * values, axis=1, keepdims=True) / D - mean_value * mean_value
    return (values - mean_value) * lax.rsqrt(spread + EPS_NORM)


def kernel(
    hid_ref, mod_ref, wp_ref, emb_ref, slot_ref, lat_ref, win_ref, wout_ref, nh_ref,
    noisy_ref, rowlat_ref, alpha_ref, kern_ref, swap_ref,
    stepped_ref, preview_ref,
    mrecv, psend, precv, asend, arecv, adp, adf, rows_s, hall, hid_t, nin, w1, w_all,
    swap_s, qkv, heads, att_s, opp_s, opp_r, rsend, rrecv, resid_s, nmx, osend, orecv,
    nimg, nimg_w, band_s, sig_s,
    p1s, p1r, p2s, p2r, p4s, p4r, p5s, p5r, hs, hr, s1s, s1r, s3s, s3r, s4s, s4r,
    rss, rsr, exs, exr, fs, fr,
):
    r = lax.axis_index("row")
    x = lax.axis_index("col")
    y, z, c = r // (NZ * 2), (r // 2) % NZ, r % 2
    right, left = (x + 1) % NX, (x + 3) % NX

    def remote(src, dst, ss, rs, tx, ty, tz, tc):
        return pltpu.make_async_remote_copy(
            src_ref=src, dst_ref=dst, send_sem=ss, recv_sem=rs,
            device_id={"row": (ty * NZ + tz) * 2 + tc, "col": tx}, device_id_type=MESH,
        )

    sent = []

    def go(copy):
        copy.start()
        sent.append(copy)
        return copy

    barrier = pltpu.get_barrier_semaphore()

    def greet(tx, ty, tz, tc):
        pl.semaphore_signal(
            barrier, inc=1, device_id={"row": (ty * NZ + tz) * 2 + tc, "col": tx}, device_id_type=MESH
        )

    for d in range(8):
        for f in range(2):
            if d or f:
                greet(x, y, (z + d) % NZ, (c + f) % 2)
            if d:
                greet(x, (y + d) % NY, z, (c + f) % 2)
    for d in range(1, 4):
        greet((x + d) % NX, y, z, c)
    pl.semaphore_wait(barrier, 32)

    line_mod = []
    for d in range(8):
        for f in range(2):
            if d or f:
                tz = (z + d) % NZ
                line_mod.append(go(remote(
                    mod_ref.at[tz], mrecv.at[z * 2 + c], p1s.at[d * 2 + f], p1r.at[d * 2 + f],
                    x, y, tz, (c + f) % 2)))
    mrecv[z * 2 + c] = mod_ref[z]

    for t in range(4):
        hall[x, :, t * COLS:(t + 1) * COLS] = hid_ref[t * TILE:(t + 1) * TILE, :]

    def hidden_copy(block, first, sem, tx):
        place = hall.at[block, pl.ds(first, 64)]
        return remote(place, place, hs.at[sem], hr.at[sem], tx, y, z, c)

    h_r0 = go(hidden_copy(x, 0, 0, right))
    h_l1 = go(hidden_copy(x, 64, 2, left))
    h_r1 = go(hidden_copy(x, 64, 1, right))
    h_l0 = go(hidden_copy(x, 0, 3, left))

    own_core = x % 2
    is_b = x // 2
    spot = z * (1 - is_b) + y * is_b
    block_id = y * (1 - is_b) + z * is_b
    owner = c == own_core

    def line_weight(d, sem):
        return remote(
            wp_ref, w1.at[spot * 2 + c], s1s.at[d], s1r.at[sem],
            x, (y + d * is_b) % NY, (z + d * (1 - is_b)) % NZ, own_core)

    for d in range(1, 8):
        go(line_weight(d, d * 2 + c))

    @pl.when(c != own_core)
    def _():
        line_weight(0, 0).start()

    @pl.when(owner)
    def _():
        w1[spot * 2 + c] = wp_ref[...]

    table = emb_ref[y].astype(F32)
    table = (table / (1.0 + jnp.exp(-table))).astype(BF16)
    lat_steps = lat_ref[5].astype(F32)
    slot_steps = jnp.sum(
        jnp.where(slot_ref[...] == iota((256, 512), 1), lat_steps, 0.0), axis=1, keepdims=True)
    slot_hot = (slot_steps == iota((256, 64), 1).astype(F32)).astype(F32).astype(BF16)
    rows_s[...] = dot(slot_hot, table).astype(BF16)

    for copy in line_mod:
        copy.wait_recv()
    part = dot(rows_s[pl.ds(pl.multiple_of(c * 128, 128), 128), :], mrecv[...].reshape(256, COLS))
    psend[...] = part.astype(BF16).reshape(8, 16, COLS)
    line_part = []
    for d in range(1, 8):
        ty = (y + d) % NY
        line_part.append(go(remote(psend.at[ty], precv.at[y], p2s.at[d], p2r.at[d], x, ty, z, c)))
    precv[y] = psend[y]

    h_r0.wait_recv()
    h_fr = go(hidden_copy(left, 0, 4, right))
    h_l1.wait_recv()
    h_fl = go(hidden_copy(right, 64, 5, left))

    def weight_x(shard, block, first, count, sem, tx):
        place = w_all.at[shard, block, pl.ds(first, count)]
        return remote(place, place, s3s.at[sem], s3r.at[sem], tx, y, z, c)

    @pl.when(owner)
    def _():
        for d in range(1, 8):
            for k in range(2):
                line_weight(d, d * 2 + k).wait_recv()
        line_weight(0, 0).wait_recv()
        keep_row = iota((BLOCK, 256), 0)
        keep_col = iota((BLOCK, 256), 1)
        keep = jnp.zeros((BLOCK, 256), F32)
        for k in range(16):
            inside = (keep_row >= k * ROWS) & (keep_row < (k + 1) * ROWS)
            keep = keep + jnp.where(inside & (keep_col == keep_row + k * (16 - ROWS)), 1.0, 0.0)
        w_all[is_b, block_id] = dot(keep.astype(BF16), w1[...].reshape(256, D)).astype(BF16)
        weight_x(is_b, block_id, 0, 80, 0, right).start()
        weight_x(is_b, block_id, 80, 64, 2, left).start()
        weight_x(is_b, block_id, 80, 64, 1, right).start()
        weight_x(is_b, block_id, 0, 80, 3, left).start()

    for copy in line_part:
        copy.wait_recv()
    total = jnp.sum(precv[...].astype(F32), axis=0)
    asend[...] = jnp.zeros((8, 8, COLS), F32)
    for k in range(8):
        asend[k, 0:2, :] = total[2 * k:2 * k + 2, :]
    line_rows = []
    for d in range(1, 8):
        tz = (z + d) % NZ
        line_rows.append(go(remote(asend.at[tz], arecv.at[z], p4s.at[d], p4r.at[d], x, y, tz, c)))
    arecv[z] = asend[z]

    from_left = left // 2
    from_right = right // 2
    block_l = y * (1 - from_left) + z * from_left
    block_r = y * (1 - from_right) + z * from_right

    @pl.when(c != own_core)
    def _():
        weight_x(from_left, block_l, 0, 80, 0, right).wait_recv()
        weight_x(from_left, block_l, 0, 80, 4, right).start()
        weight_x(from_right, block_r, 80, 64, 2, left).wait_recv()
        weight_x(from_right, block_r, 80, 64, 5, left).start()
        weight_x(from_left, block_l, 80, 64, 1, right).wait_recv()
        weight_x(from_right, block_r, 0, 80, 3, left).wait_recv()

    other = 1 - is_b
    block_o = y * (1 - other) + z * other

    @pl.when(owner)
    def _():
        weight_x(other, block_o, 0, 80, 4, right).wait_recv()
        weight_x(other, block_o, 80, 64, 5, left).wait_recv()

    def ring_copy(g, way, t, k):
        p = y if g == 0 else z
        step = 1 if way == 0 else 7
        block = (p + t * (8 - step)) % 8
        first, count = CHUNKS[k]
        place = w_all.at[g, block, pl.ds(first, count)]
        sem = ((g * 2 + way) * 4 + t) * 4 + k
        ty = (y + step) % NY if g == 0 else y
        tz = (z + step) % NZ if g == 1 else z
        return remote(place, place, s4s.at[sem], s4r.at[sem], x, ty, tz, c)

    def ring_chunks(way, t):
        if way == 0:
            return (0, 1, 2, 3) if t < 3 else (0, 1)
        return (2, 3, 0, 1) if t < 3 else (2, 3)

    ring = {}
    for slot in range(4):
        for g in range(2):
            for way in range(2):
                k = ring_chunks(way, 0)[slot]
                ring[g, way, 0, k] = go(ring_copy(g, way, 0, k))
    pending = []
    for t in range(1, 4):
        for slot in range(len(ring_chunks(0, t))):
            for g in range(2):
                for way in range(2):
                    pending.append((g, way, t, ring_chunks(way, t)[slot]))
    waited = set()

    def pump(count):
        for _ in range(min(count, len(pending))):
            g, way, t, k = pending.pop(0)
            ring[g, way, t - 1, k].wait_recv()
            waited.add((g, way, t - 1, k))
            ring[g, way, t, k] = go(ring_copy(g, way, t, k))

    h_r1.wait_recv()
    h_l0.wait_recv()
    h_fr.wait_recv()
    h_fl.wait_recv()
    for t in range(4):
        for k in range(4):
            hid_t[t, :, k * COLS:(k + 1) * COLS] = hall[k, :, t * COLS:(t + 1) * COLS]

    for copy in line_rows:
        copy.wait_recv()
    for k in range(8):
        adp[x, 2 * k:2 * k + 2, :] = arecv[k, 0:2, :]
    adp[x, 16:32, :] = nh_ref[...]
    cross = []
    for d in range(1, 4):
        tx = (x + d) % NX
        cross.append(go(remote(adp.at[x], adp.at[x], p5s.at[d], p5r.at[d], tx, y, z, c)))

    for k in range(9):
        rows = slice(k * 128, (k + 1) * 128)
        swap_s[rows, :] = (swap_ref[rows, :] == iota((128, D), 1)).astype(F32).astype(BF16)
    spread_out = (iota((4, 128), 0) == iota((4, 128), 1) % 4).astype(F32)
    wide = exact_dot(kern_ref[...], spread_out)
    pixel_gap = iota((128, 128), 0) // 4 - iota((128, 128), 1) // 4
    for k in range(3):
        band = jnp.zeros((128, 128), F32)
        for off in range(3):
            base = (k * 3 + off) * 4
            pick = (iota((128, 36), 1) == base + iota((128, 36), 0) % 4).astype(F32)
            band = band + jnp.where(pixel_gap == off - 1, exact_dot(pick, wide), 0.0)
        band_s[k] = band

    for copy in cross:
        copy.wait_recv()
    for k in range(4):
        adf[:, k * COLS:(k + 1) * COLS] = adp[k]

    last_lat = lat_ref[3, :, 0:1]

    def rows_of(tile, which):
        later = (lat_ref[tile, :, 0:1] == last_lat).astype(F32)
        return later * adf[2 * which + 1:2 * which + 2, :] + (1.0 - later) * adf[2 * which:2 * which + 1, :]

    for t in range(4):
        values = normalized(hid_t[t].astype(F32))
        nin[t] = (values * (1.0 + rows_of(t, 1)) + rows_of(t, 0)).astype(BF16)
        for s in range(3):
            qkv[s, t] = dot(nin[t], win_ref[s]).astype(BF16)
        pump(2)
    for s in range(3):
        for h in range(HEADS_HERE):
            for t in range(4):
                heads[s, h, t] = qkv[s, t, :, h * HEAD_DIM:(h + 1) * HEAD_DIM]

    scale_factor = HEAD_DIM ** (-0.5)

    def attend(tile):
        allowed = lat_ref[4] == lat_ref[tile]
        for h in range(HEADS_HERE):
            keys = heads[1, h].reshape(512, HEAD_DIM)
            mates = heads[2, h].reshape(512, HEAD_DIM)
            scores = dot_nt(heads[0, h, tile], keys) * scale_factor
            scores = jnp.where(allowed, scores, -1e30)
            raised = jnp.exp(scores - jnp.max(scores, axis=1, keepdims=True))
            weights = raised / jnp.sum(raised, axis=1, keepdims=True)
            mixed = dot(weights.astype(BF16), mates)
            att_s[:, h * HEAD_DIM:(h + 1) * HEAD_DIM] = mixed.astype(BF16)
        return dot(att_s[...], wout_ref[...]).astype(BF16)

    opp_s[...] = attend((x + 2) % NX)
    opp_right = go(remote(opp_s.at[pl.ds(0, 64)], opp_r.at[0], rss.at[0], rsr.at[0], right, y, z, c))
    opp_left = go(remote(opp_s.at[pl.ds(64, 64)], opp_r.at[1], rss.at[1], rsr.at[1], left, y, z, c))
    pump(4)
    rsend[0] = attend(right)
    pump(4)
    opp_right.wait_recv()
    rsend[0, 0:64] = (rsend[0, 0:64].astype(F32) + opp_r[0].astype(F32)).astype(BF16)
    to_right = go(remote(rsend.at[0], rrecv.at[0], rss.at[2], rsr.at[2], right, y, z, c))
    rsend[1] = attend(left)
    pump(4)
    opp_left.wait_recv()
    rsend[1, 64:128] = (rsend[1, 64:128].astype(F32) + opp_r[1].astype(F32)).astype(BF16)
    to_left = go(remote(rsend.at[1], rrecv.at[1], rss.at[3], rsr.at[3], left, y, z, c))
    mine = attend(x).astype(F32)
    pump(8)
    to_right.wait_recv()
    to_left.wait_recv()
    attn_sum = mine + rrecv[0].astype(F32) + rrecv[1].astype(F32)
    residual = (hid_t[x].astype(F32) + rows_of(x, 2) * attn_sum).astype(BF16)
    resid_s[...] = residual
    values = normalized(residual.astype(F32))
    nmx[c] = (values * (1.0 + rows_of(x, 4)) + rows_of(x, 3)).astype(BF16)
    swap_mid = go(remote(nmx.at[c], nmx.at[c], exs.at[0], exr.at[0], x, y, z, 1 - c))
    pump(len(pending))
    swap_mid.wait_recv()
    both = nmx[...].reshape(256, D)
    for key, copy in ring.items():
        if key not in waited:
            copy.wait_recv()
    both_swapped = dot(both, swap_s[...]).astype(BF16)

    def mlp(g, features):
        packed = w_all.at[g]
        expanded = dot(features, packed[:, :, 512:D].reshape(D, D - 512))[:, 64:64 + UNITS]
        activated = jax.nn.gelu(expanded, approximate=True).astype(BF16)
        return dot_nt(activated, packed[:, :, 0:UNITS].reshape(D, UNITS)).astype(BF16)

    mlp_part = mlp(0, both).astype(F32) + dot(mlp(1, both_swapped), swap_s[...])
    osend[...] = mlp_part.reshape(2, TILE, D)
    swap_out = go(remote(osend.at[1 - c], orecv, exs.at[1], exr.at[1], x, y, z, 1 - c))

    row_lat = rowlat_ref[...]
    row_steps = jnp.sum(
        jnp.where(row_lat == iota((64, 512), 1), lat_steps, 0.0), axis=1, keepdims=True)
    row_hot = row_steps == iota((64, 128), 1).astype(F32)
    signal_now = jnp.sum(jnp.where(row_hot, alpha_ref[0:1, :], 0.0), axis=1, keepdims=True)
    signal_next = jnp.sum(jnp.where(row_hot, alpha_ref[1:2, :], 0.0), axis=1, keepdims=True)
    head_rows = jnp.concatenate([adf[16:24, :]] * 16 + [adf[24:32, :]] * 16, axis=0).astype(BF16)

    swap_out.wait_recv()
    mlp_sum = osend[c] + orecv[...]
    second = (resid_s[...].astype(F32) + rows_of(x, 5) * mlp_sum).astype(BF16)
    values = normalized(second.astype(F32))
    normed_out = (values * (1.0 + rows_of(x, 7)) + rows_of(x, 6)).astype(BF16)
    noise = dot_nt(normed_out, head_rows)
    token_col = iota((TILE, 256), 0) % GRIDW
    lane_col = (iota((TILE, 256), 1) % 128) // 8
    noise = jnp.where(token_col == lane_col, noise, 0.0)
    noise = jnp.sum(noise.reshape(8, GRIDW, 256), axis=1)
    nimg_w[pl.ds(0, 8, 2), :] = noise[:, 0:128]
    nimg_w[pl.ds(1, 8, 2), :] = noise[:, 128:256]
    nimg[x] = nimg_w[...]
    last = []
    for d in range(1, 4):
        tx = (x + d) % NX
        last.append(go(remote(nimg.at[x], nimg.at[x], fs.at[d], fr.at[d], tx, y, z, c)))
    for copy in last:
        copy.wait_recv()
    noise_img = nimg[...].reshape(64, 128)
    clean = (noisy_ref[...].astype(F32) - jnp.sqrt(1.0 - signal_now) * noise_img) / jnp.sqrt(signal_now)
    stepped_ref[...] = (
        jnp.sqrt(signal_next) * clean + jnp.sqrt(1.0 - signal_next) * noise_img).astype(BF16)
    blank = jnp.zeros((1, 128), F32)
    above = jnp.concatenate([blank, clean[:-1]], axis=0)
    below = jnp.concatenate([clean[1:], blank], axis=0)
    no_row = jnp.full((1, 1), -1.0, F32)
    lat_f = row_lat.astype(F32)
    above_ok = jnp.concatenate([no_row, lat_f[:-1]], axis=0) == lat_f
    below_ok = jnp.concatenate([lat_f[1:], no_row], axis=0) == lat_f
    preview = (
        jnp.where(above_ok, exact_dot(above, band_s[0]), 0.0)
        + exact_dot(clean, band_s[1])
        + jnp.where(below_ok, exact_dot(below, band_s[2]), 0.0)
    )
    preview_ref[...] = preview.astype(BF16)

    for copy in sent:
        copy.wait_send()

    @pl.when(c != own_core)
    def _():
        line_weight(0, 0).wait_send()
        weight_x(from_left, block_l, 0, 80, 4, right).wait_send()
        weight_x(from_right, block_r, 80, 64, 5, left).wait_send()

    @pl.when(owner)
    def _():
        weight_x(is_b, block_id, 0, 80, 0, right).wait_send()
        weight_x(is_b, block_id, 80, 64, 2, left).wait_send()
        weight_x(is_b, block_id, 80, 64, 1, right).wait_send()
        weight_x(is_b, block_id, 0, 80, 3, left).wait_send()


def shards(
    hidden, noisy_latent, tile_latent, timesteps, step_embedding, alpha_now, alpha_next,
    modulation, attention_in, attention_out, expand_weight, reduce_weight, noise_head, preview_kernel,
):
    r = lax.axis_index("row")
    my_latent = lax.dynamic_slice_in_dim(tile_latent, r * 4, 4)
    mod = jnp.pad(modulation.transpose(1, 0, 2), ((0, 0), (0, 16 - ROWS), (0, 0)))
    packed = jnp.pad(
        jnp.concatenate([reduce_weight.T, expand_weight], axis=1), ((0, 16 - ROWS), (0, 0)))
    emb = jnp.pad(
        step_embedding.reshape(STEPS, NY, 16, ROWS), ((0, 14), (0, 0), (0, 0), (0, 16 - ROWS)))
    emb = emb.transpose(1, 0, 2, 3).reshape(NY, 64, 256)
    slots = tile_latent.reshape(NY, NZ, 2, 4)[:, :, :, 0::3].transpose(2, 0, 1, 3).reshape(256, 1)
    lat = jnp.concatenate([
        jnp.broadcast_to(my_latent[:, None], (4, 512)),
        jnp.repeat(my_latent, TILE)[None, :],
        timesteps[None, :],
        jnp.zeros((2, 512), jnp.int32),
    ], axis=0)[:, None, :]
    row_lat = jnp.repeat(my_latent, 16)[:, None]
    alphas = jnp.pad(jnp.stack([alpha_now, alpha_next]), ((0, 6), (0, 128 - STEPS)))
    win = attention_in.transpose(1, 0, 2)
    head = noise_head.T.astype(F32)
    kern = preview_kernel.reshape(36, 4)
    swap = jnp.asarray(swapped_order())
    vmem = pl.BlockSpec(memory_space=pltpu.VMEM)
    dma = pltpu.SemaphoreType.DMA
    return pl.pallas_call(
        kernel,
        out_shape=(jax.ShapeDtypeStruct((64, 128), BF16), jax.ShapeDtypeStruct((64, 128), BF16)),
        in_specs=[vmem] * 14,
        out_specs=(vmem, vmem),
        scratch_shapes=[
            pltpu.VMEM((16, 16, COLS), BF16),
            pltpu.VMEM((8, 16, COLS), BF16),
            pltpu.VMEM((8, 16, COLS), BF16),
            pltpu.VMEM((8, 8, COLS), F32),
            pltpu.VMEM((8, 8, COLS), F32),
            pltpu.VMEM((4, 32, COLS), F32),
            pltpu.VMEM((32, D), F32),
            pltpu.VMEM((256, 256), BF16),
            pltpu.VMEM((4, TILE, D), BF16),
            pltpu.VMEM((4, TILE, D), BF16),
            pltpu.VMEM((4, TILE, D), BF16),
            pltpu.VMEM((16, 16, D), BF16),
            pltpu.VMEM((2, 8, BLOCK, D), BF16),
            pltpu.VMEM((D, D), BF16),
            pltpu.VMEM((3, 4, TILE, COLS), BF16),
            pltpu.VMEM((3, HEADS_HERE, 4, TILE, HEAD_DIM), BF16),
            pltpu.VMEM((TILE, COLS), BF16),
            pltpu.VMEM((TILE, D), BF16),
            pltpu.VMEM((2, 64, D), BF16),
            pltpu.VMEM((2, TILE, D), BF16),
            pltpu.VMEM((2, TILE, D), BF16),
            pltpu.VMEM((TILE, D), BF16),
            pltpu.VMEM((2, TILE, D), BF16),
            pltpu.VMEM((2, TILE, D), F32),
            pltpu.VMEM((TILE, D), F32),
            pltpu.VMEM((4, 16, 128), F32),
            pltpu.VMEM((16, 128), F32),
            pltpu.VMEM((3, 128, 128), F32),
            pltpu.VMEM((64, 128), F32),
            dma((16,)), dma((16,)),
            dma((8,)), dma((8,)),
            dma((8,)), dma((8,)),
            dma((4,)), dma((4,)),
            dma((6,)), dma((6,)),
            dma((8,)), dma((16,)),
            dma((6,)), dma((6,)),
            dma((64,)), dma((64,)),
            dma((4,)), dma((4,)),
            dma((2,)), dma((2,)),
            dma((4,)), dma((4,)),
        ],
        compiler_params=pltpu.CompilerParams(
            collective_id=0, has_side_effects=True, vmem_limit_bytes=60 * 1024 * 1024),
        name="dit_block",
    )(hidden, mod, packed, emb, slots, lat, win, attention_out, head, noisy_latent, row_lat, alphas, kern, swap)


def solution(mesh):
    return jax.shard_map(
        shards,
        mesh=mesh,
        in_specs=(
            P("row", "col"),
            P("row", None),
            P(),
            P(),
            P(),
            P(),
            P(),
            P("row", None, "col"),
            P(None, None, "col"),
            P("col", None),
            P("row", "col"),
            P("col", "row"),
            P("col", None),
            P(),
        ),
        out_specs=(P("row", None), P("row", None)),
        check_vma=False,
    )
```

```python
import functools

import jax
import jax.numpy as jnp
from jax import lax
from jax.experimental import pallas as pl
from jax.experimental.pallas import tpu as pltpu
from jax.sharding import PartitionSpec as P

D = 1152
HEAD_DIM = 72
HEADS_HERE = 4
GRIDW = 16
STEPS = 50
TILE = 128
NX, NY, NZ = 4, 8, 8
COLS = D // NX
UNITS = 2304 // NX
ROWS = 9
BLOCK = 144
EPS_NORM = 1e-06
MESH = pl.DeviceIdType.MESH
F32 = jnp.float32
BF16 = jnp.bfloat16
CHUNKS = ((0, 48), (48, 32), (80, 32), (112, 32))


def swap_column(first, count):
    index = (iota((count, 1), 0) + first).astype(F32)
    major = jnp.floor((index + 0.5) * (1.0 / 144.0))
    rest = index - major * 144.0
    minor = jnp.floor((rest + 0.5) * (1.0 / 18.0))
    return minor * 144.0 + major * 18.0 + (rest - minor * 18.0)


def iota(shape, dim):
    return lax.broadcasted_iota(jnp.int32, shape, dim)


def dot(a, b):
    return jnp.dot(a, b, preferred_element_type=F32)


def dot_nt(a, b):
    return lax.dot_general(a, b, (((1,), (1,)), ((), ())), preferred_element_type=F32)


def dot_tn(a, b):
    return lax.dot_general(a, b, (((0,), (0,)), ((), ())), preferred_element_type=F32)


def exact_dot(a, b):
    return jnp.dot(a, b, preferred_element_type=F32, precision=lax.Precision.HIGHEST)


def normalized(values):
    mean_value = jnp.sum(values, axis=1, keepdims=True) / D
    spread = jnp.sum(values * values, axis=1, keepdims=True) / D - mean_value * mean_value
    return (values - mean_value) * lax.rsqrt(spread + EPS_NORM)


def kernel(
    hid_ref, mod_ref, red_ref, exp_ref, emb_ref, tl_ref, ts_ref, win_ref, wout_ref, nh_ref,
    noisy_ref, now_ref, next_ref, kern_ref,
    out_ref,
    mod_s, wp_s, mrecv, psend, precv, asend, arecv, adp_s, adp, adf, nh_s, rows_s, hall, norm_s, nin, w1, w_all,
    win_s, wout_s, swap_s, qkv, keys_s, att_s, lat_s, rsend, rrecv, hid_s, resid_s, nmx, osend, orecv,
    nimg, nimg_w, band_s,
    p1s, p1r, p2s, p2r, p4s, p4r, p5s, p5r, nhs, nhr, los, hs, hr, s1s, s1r, s3s, s3r, s4s, s4r,
    wxs, wxr, rss, rsr, exs, exr, fs, fr,
):
    r = lax.axis_index("row")
    x = lax.axis_index("col")
    y, z, c = r // (NZ * 2), (r // 2) % NZ, r % 2
    right, left = (x + 1) % NX, (x + 3) % NX

    def remote(src, dst, ss, rs, tx, ty, tz, tc):
        return pltpu.make_async_remote_copy(
            src_ref=src, dst_ref=dst, send_sem=ss, recv_sem=rs,
            device_id={"row": (ty * NZ + tz) * 2 + tc, "col": tx}, device_id_type=MESH,
        )

    sent = []

    def go(copy):
        copy.start()
        sent.append(copy)
        return copy

    win_load = pltpu.make_async_copy(win_ref, win_s, los.at[0])
    wout_load = pltpu.make_async_copy(wout_ref, wout_s.at[x], los.at[1])
    win_load.start()
    wout_load.start()
    barrier = pltpu.get_barrier_semaphore()

    def greet(tx, ty, tz, tc):
        pl.semaphore_signal(
            barrier, inc=1, device_id={"row": (ty * NZ + tz) * 2 + tc, "col": tx}, device_id_type=MESH
        )

    for d in range(8):
        for f in range(2):
            if d or f:
                greet(x, y, (z + d) % NZ, (c + f) % 2)
            if d:
                greet(x, (y + d) % NY, z, (c + f) % 2)
    for d in range(1, 4):
        for f in range(2):
            greet((x + d) % NX, y, z, (c + f) % 2)
    slab = (iota((128, 72), 0) % 16) * 8 + iota((128, 72), 0) // 16
    slab = jnp.where(iota((128, 72), 0) % 16 < ROWS, slab, -1)
    pick_mod = (slab == iota((128, 72), 1)).astype(F32).astype(BF16)
    mod_rows = mod_ref[...].astype(F32).reshape(72, COLS).astype(BF16)
    mod_s[...] = dot(pick_mod, mod_rows).astype(BF16).reshape(8, 16, COLS)
    pack = jnp.concatenate([red_ref[...].astype(F32), exp_ref[...].astype(F32)], axis=1)
    spare = jnp.concatenate([pack[7:9, 768:D], jnp.zeros((5, 384), F32)], axis=0)
    spare = jnp.concatenate([pack[0:7, 768:D], spare], axis=1)
    wp_s[...] = jnp.concatenate([pack[:, 0:768], spare], axis=0).astype(BF16)
    pl.semaphore_wait(barrier, 35)

    line_mod = []
    for d in range(1, 8):
        tz = (z + d) % NZ
        line_mod.append(go(remote(mod_s.at[tz], mrecv.at[z], p1s.at[d], p1r.at[d], x, y, tz, c)))
    mrecv[z] = mod_s[z]

    def hidden_copy(block, first, sem, tx):
        rows = pl.ds(first, 144)
        src = hid_ref.at[rows] if block is x else hall.at[block, rows]
        return remote(src, hall.at[block, rows], hs.at[sem], hr.at[sem], tx, y, z, c)

    h_r0 = go(hidden_copy(x, 0, 0, right))
    h_l1 = go(hidden_copy(x, 144, 2, left))
    h_r1 = go(hidden_copy(x, 144, 1, right))
    h_l0 = go(hidden_copy(x, 0, 3, left))
    hall[x] = hid_ref[...]
    heads = []
    for d in range(1, 4):
        heads.append(go(remote(nh_ref, nh_s.at[x], nhs.at[d], nhr.at[d], (x + d) % NX, y, z, c)))
    nh_s[x] = nh_ref[...]

    own_core = x % 2
    is_b = x // 2
    spot = z * (1 - is_b) + y * is_b
    block_id = y * (1 - is_b) + z * is_b
    owner = c == own_core

    def line_weight(d, sem):
        return remote(
            wp_s, w1.at[spot * 2 + c], s1s.at[d], s1r.at[sem],
            x, (y + d * is_b) % NY, (z + d * (1 - is_b)) % NZ, own_core)

    for d in range(1, 8):
        go(line_weight(d, d * 2 + c))

    @pl.when(c != own_core)
    def _():
        line_weight(0, 0).start()

    @pl.when(owner)
    def _():
        w1[spot * 2 + c] = wp_s[...]

    tile_lat = tl_ref[...].astype(F32)
    lat_steps = ts_ref[...].astype(F32)

    def looked_up(where_to, values):
        return jnp.sum(jnp.where(where_to, values, 0.0), axis=1, keepdims=True)

    table = emb_ref[...].astype(F32)
    table = (table / (1.0 + jnp.exp(-table))).astype(BF16)
    slot_col = iota((D, 128), 1)
    from_row = jnp.where(
        slot_col % 16 < ROWS, y * BLOCK + ((slot_col // 16) * 2 + c) * ROWS + slot_col % 16, -1)
    table = dot(table, (iota((D, 128), 0) == from_row).astype(F32).astype(BF16)).astype(BF16)
    slot = iota((256, 512), 0)
    slot_tile = (slot // 2) * 4 + 3 * (slot % 2)
    lane512 = iota((256, 512), 1)
    slot_lat = looked_up(slot_tile == lane512, tile_lat)
    slot_steps = looked_up(slot_lat == lane512.astype(F32), lat_steps)
    slot_hot = (slot_steps == iota((256, STEPS), 1).astype(F32)).astype(F32).astype(BF16)
    rows_s[...] = dot(slot_hot, table).astype(BF16)
    row_lat = looked_up(iota((64, 512), 1) == r * 4 + iota((64, 512), 0) // 16, tile_lat)
    for t in range(4):
        lat_s[t] = jnp.broadcast_to(row_lat[16 * t:16 * t + 1, :], (1, 128))

    for copy in line_mod:
        copy.wait_recv()
    part = dot(rows_s[...], mrecv[...].reshape(128, COLS))
    psend[...] = part.astype(BF16).reshape(8, 32, COLS)
    line_part = []
    for d in range(1, 8):
        ty = (y + d) % NY
        line_part.append(go(remote(psend.at[ty], precv.at[y], p2s.at[d], p2r.at[d], x, ty, z, c)))
    precv[y] = psend[y]

    h_r0.wait_recv()
    h_fr = go(hidden_copy(left, 0, 4, right))
    h_l1.wait_recv()
    h_fl = go(hidden_copy(right, 144, 5, left))

    def ring_copy(g, way, t, k):
        p = y * (1 - g) + z * g
        step = 1 if way == 0 else 7
        block = (p + t * (8 - step)) % 8
        first, count = CHUNKS[k]
        place = w_all.at[g, block, pl.ds(first, count)]
        sem = ((g * 2 + way) * 4 + t) * 4 + k
        return remote(
            place, place, s4s.at[sem], s4r.at[sem],
            x, (y + step * (1 - g)) % NY, (z + step * g) % NZ, c)

    def ring_chunks(way, t):
        if way == 0:
            return (0, 1, 2, 3) if t < 3 else (0, 1)
        return (2, 3, 0, 1) if t < 3 else (2, 3)

    def ring_start(g):
        for slot in range(4):
            for way in range(2):
                ring_copy(g, way, 0, ring_chunks(way, 0)[slot]).start()

    def weight_x(shard, block, first, count, sem, tx):
        place = w_all.at[shard, block, pl.ds(first, count)]
        return remote(place, place, s3s.at[sem], s3r.at[sem], tx, y, z, c)

    @pl.when(owner)
    def _():
        for d in range(1, 8):
            for k in range(2):
                line_weight(d, d * 2 + k).wait_recv()
        line_weight(0, 0).wait_recv()
        keep_row = iota((BLOCK, 256), 0)
        keep_col = iota((BLOCK, 256), 1)
        source = jnp.zeros((BLOCK, 256), jnp.int32)
        for k in range(1, 16):
            source = source + jnp.where(keep_row >= k * ROWS, 16 - ROWS, 0)
        word = keep_row + source - jnp.where(source >= 0, (source // (16 - ROWS)) * 16, 0)
        source = source + keep_row

        def picked(offset, valid):
            hit = (keep_col == source + offset) & valid
            return jnp.where(hit, 1.0, 0.0).astype(BF16)

        lines = w1[...].reshape(256, 768)
        w_all[is_b, block_id, :, 0:768] = dot(picked(0, word >= 0), lines).astype(BF16)
        w_all[is_b, block_id, :, 768:D] = (
            dot(picked(ROWS, word < 7), lines[:, 0:384])
            + dot(picked(ROWS - 7, word >= 7), lines[:, 384:768])).astype(BF16)
        weight_x(is_b, block_id, 0, 80, 0, right).start()
        weight_x(is_b, block_id, 80, 64, 2, left).start()
        weight_x(is_b, block_id, 80, 64, 1, right).start()
        weight_x(is_b, block_id, 0, 80, 3, left).start()
        ring_start(is_b)

    spread_out = (iota((4, 128), 0) == iota((4, 128), 1) % 4).astype(F32)
    gather_in = (iota((128, 4), 1) == iota((128, 4), 0) % 4).astype(F32)
    pixel_gap = iota((128, 128), 0) // 4 - iota((128, 128), 1) // 4
    for k in range(3):
        band = jnp.zeros((128, 128), F32)
        for off in range(3):
            full = exact_dot(gather_in, exact_dot(kern_ref[k, off], spread_out))
            band = band + jnp.where(pixel_gap == off - 1, full, 0.0)
        band_s[k] = band

    for copy in line_part:
        copy.wait_recv()
    total = jnp.sum(precv[...].astype(F32), axis=0)
    asend[...] = jnp.zeros((8, 8, COLS), F32)
    for k in range(8):
        asend[k, 0:4, :] = total[4 * k:4 * k + 4, :]
    line_rows = []
    for d in range(1, 8):
        tz = (z + d) % NZ
        line_rows.append(go(remote(asend.at[tz], arecv.at[z], p4s.at[d], p4r.at[d], x, y, tz, c)))
    arecv[z] = asend[z]

    from_left = left // 2
    from_right = right // 2
    block_l = y * (1 - from_left) + z * from_left
    block_r = y * (1 - from_right) + z * from_right

    @pl.when(c != own_core)
    def _():
        weight_x(from_left, block_l, 0, 80, 0, right).wait_recv()
        weight_x(from_left, block_l, 0, 80, 4, right).start()
        weight_x(from_right, block_r, 80, 64, 2, left).wait_recv()
        weight_x(from_right, block_r, 80, 64, 5, left).start()
        weight_x(from_left, block_l, 80, 64, 1, right).wait_recv()
        weight_x(from_right, block_r, 0, 80, 3, left).wait_recv()
        ring_start(0)
        ring_start(1)

    other = 1 - is_b
    block_o = y * (1 - other) + z * other

    @pl.when(owner)
    def _():
        weight_x(other, block_o, 0, 80, 4, right).wait_recv()
        weight_x(other, block_o, 80, 64, 5, left).wait_recv()
        ring_start(other)

    def wout_x(shard, first, count, sem, tx):
        place = wout_s.at[shard, c, pl.ds(first, count)]
        return remote(place, place, wxs.at[sem], wxr.at[sem], tx, y, z, c)

    wout_load.wait()
    o_r0 = go(wout_x(x, 0, 80, 0, right))
    o_l1 = go(wout_x(x, 80, 64, 2, left))
    o_r1 = go(wout_x(x, 80, 64, 1, right))
    o_l0 = go(wout_x(x, 0, 80, 3, left))

    ring = {}
    for g in range(2):
        for way in range(2):
            for k in ring_chunks(way, 0):
                ring[g, way, 0, k] = ring_copy(g, way, 0, k)
                sent.append(ring[g, way, 0, k])
    pending = []
    for t in range(1, 4):
        for slot in range(len(ring_chunks(0, t))):
            for g in range(2):
                for way in range(2):
                    pending.append((g, way, t, ring_chunks(way, t)[slot]))
    waited = set()

    def pump(count):
        for _ in range(min(count, len(pending))):
            g, way, t, k = pending.pop(0)
            ring[g, way, t - 1, k].wait_recv()
            waited.add((g, way, t - 1, k))
            ring[g, way, t, k] = go(ring_copy(g, way, t, k))

    h_r1.wait_recv()
    h_l0.wait_recv()
    h_fr.wait_recv()
    h_fl.wait_recv()
    for t in range(4):
        values = hall[:, :, t * TILE:(t + 1) * TILE].reshape(D, TILE).astype(F32)
        mean_value = jnp.sum(values, axis=0, keepdims=True) / D
        spread = jnp.sum(values * values, axis=0, keepdims=True) / D - mean_value * mean_value
        norm_s[:, t * TILE:(t + 1) * TILE] = (values - mean_value) * lax.rsqrt(spread + EPS_NORM)

    for copy in line_rows:
        copy.wait_recv()
    for k in range(8):
        for f in range(2):
            adp_s[f, 2 * k:2 * k + 2, :] = arecv[k, 2 * f:2 * f + 2, :]
    cross = []
    for d in range(4):
        for f in range(2):
            if d or f:
                tc = (c + f) % 2
                cross.append(go(remote(
                    adp_s.at[tc], adp.at[x, c], p5s.at[d * 2 + f], p5r.at[d * 2 + f],
                    (x + d) % NX, y, z, tc)))
    adp[x, c] = adp_s[c]
    pump(4)

    o_r0.wait_recv()
    o_fr = go(wout_x(left, 0, 80, 4, right))
    o_l1.wait_recv()
    o_fl = go(wout_x(right, 80, 64, 5, left))
    for copy in cross:
        copy.wait_recv()
    for k in range(4):
        adf[:, k * COLS:(k + 1) * COLS] = adp[k, 0] + adp[k, 1]

    def rows_of(tile, which):
        later = (lat_s[tile, :, 0:1] == lat_s[3, :, 0:1]).astype(F32)
        return later * adf[2 * which + 1:2 * which + 2, :] + (1.0 - later) * adf[2 * which:2 * which + 1, :]

    columns = jnp.concatenate([rows_of(t, k) for k in (0, 1) for t in range(4)], axis=0).T
    for t in range(4):
        values = norm_s[:, t * TILE:(t + 1) * TILE]
        nin[:, t * TILE:(t + 1) * TILE] = (
            values * (1.0 + columns[:, 4 + t:5 + t]) + columns[:, t:t + 1]).astype(BF16)
        pump(2)
    win_load.wait()
    win = win_s[...].reshape(3 * COLS, D)
    for t in range(2):
        lanes = slice(t * 256, (t + 1) * 256)
        qkv[:, lanes] = dot(win, nin[:, lanes]).astype(BF16)
    pump(4)
    for h in range(HEADS_HERE):
        rows = slice(COLS + h * HEAD_DIM, COLS + (h + 1) * HEAD_DIM)
        keys_s[h] = qkv[rows, :].T

    def wout_core(shard, sem):
        place = wout_s.at[shard, c]
        return remote(place, place, wxs.at[sem], wxr.at[sem], x, y, z, 1 - c)

    o_r1.wait_recv()
    o_cl = go(wout_core(left, 6))
    o_l0.wait_recv()
    o_cr = go(wout_core(right, 7))

    scale_factor = HEAD_DIM ** (-0.5)

    def attend(tile):
        lanes = pl.ds(pl.multiple_of(tile * TILE, TILE), TILE)
        bias = [
            jnp.where(lat_s[u] == lat_s[tile], 0.0, -1e30) for u in range(4)]
        for h in range(HEADS_HERE):
            rows = slice(h * HEAD_DIM, (h + 1) * HEAD_DIM)
            query = qkv[rows, lanes]
            mates = qkv[2 * COLS + rows.start:2 * COLS + rows.stop, :]
            scores = dot(keys_s[h], query) * scale_factor
            scores = jnp.concatenate(
                [scores[u * TILE:(u + 1) * TILE] + bias[u] for u in range(4)], axis=0)
            raised = jnp.exp(scores - jnp.max(scores, axis=0, keepdims=True))
            share = 1.0 / jnp.sum(raised, axis=0, keepdims=True)
            att_s[rows, :] = dot(mates, raised.astype(BF16)) * share
        return att_s[...].astype(BF16)

    facing = (x + 2) % NX
    share_out = []
    for k, tile in enumerate((facing, right, left)):
        rsend[k] = attend(tile)
        share_out.append(go(remote(rsend.at[k], rrecv.at[x], rss.at[k], rsr.at[k], tile, y, z, c)))
        pump(6)
    rrecv[x] = attend(x)
    o_fr.wait_recv()
    o_fl.wait_recv()
    o_co = go(wout_core(facing, 8))
    pump(6)
    hid_s[...] = hall[:, :, pl.ds(pl.multiple_of(x * TILE, TILE), TILE)].reshape(D, TILE).astype(F32).T.astype(BF16)

    for k in range(9):
        rows = slice(k * 128, (k + 1) * 128)
        swap_s[rows, :] = (swap_column(k * 128, 128) == iota((128, D), 1).astype(F32)).astype(F32).astype(BF16)
    for copy in share_out:
        copy.wait_recv()
    o_cl.wait_recv()
    o_cr.wait_recv()
    o_co.wait_recv()
    attn_sum = dot_tn(rrecv[...].reshape(D, TILE), wout_s[...].reshape(D, D))
    residual = (hid_s[...].astype(F32) + rows_of(x, 2) * attn_sum).astype(BF16)
    resid_s[...] = residual
    values = normalized(residual.astype(F32))
    nmx[c] = (values * (1.0 + rows_of(x, 4)) + rows_of(x, 3)).astype(BF16)
    swap_mid = go(remote(nmx.at[c], nmx.at[c], exs.at[0], exr.at[0], x, y, z, 1 - c))
    pump(len(pending))
    swap_mid.wait_recv()
    both = nmx[...].reshape(256, D)
    for key, copy in ring.items():
        if key not in waited:
            copy.wait_recv()
    both_swapped = dot(both, swap_s[...]).astype(BF16)

    def mlp(g, features):
        packed = w_all.at[g]
        expanded = dot(features, packed[:, :, 512:D].reshape(D, D - 512))[:, 64:64 + UNITS]
        activated = jax.nn.gelu(expanded, approximate=True).astype(BF16)
        return dot_nt(activated, packed[:, :, 0:UNITS].reshape(D, UNITS)).astype(BF16)

    mlp_part = mlp(0, both).astype(F32) + dot(mlp(1, both_swapped), swap_s[...])
    osend[...] = mlp_part.reshape(2, TILE, D)
    swap_out = go(remote(osend.at[1 - c], orecv, exs.at[1], exr.at[1], x, y, z, 1 - c))

    row_steps = looked_up(row_lat == iota((64, 512), 1).astype(F32), lat_steps)
    row_hot = row_steps == iota((64, STEPS), 1).astype(F32)
    signal_now = looked_up(row_hot, now_ref[...])
    signal_next = looked_up(row_hot, next_ref[...])
    for copy in heads:
        copy.wait_recv()
    head = jnp.concatenate([nh_s[k].astype(F32) for k in range(4)], axis=1)
    head_rows = jnp.concatenate([head[0:8, :]] * 16 + [head[8:16, :]] * 16, axis=0).astype(BF16)

    swap_out.wait_recv()
    mlp_sum = osend[c] + orecv[...]
    second = (resid_s[...].astype(F32) + rows_of(x, 5) * mlp_sum).astype(BF16)
    values = normalized(second.astype(F32))
    normed_out = (values * (1.0 + rows_of(x, 7)) + rows_of(x, 6)).astype(BF16)
    noise = dot_nt(normed_out, head_rows)
    token_col = iota((TILE, 256), 0) % GRIDW
    lane_col = (iota((TILE, 256), 1) % 128) // 8
    noise = jnp.where(token_col == lane_col, noise, 0.0)
    noise = jnp.sum(noise.reshape(8, GRIDW, 256), axis=1)
    nimg_w[pl.ds(0, 8, 2), :] = noise[:, 0:128]
    nimg_w[pl.ds(1, 8, 2), :] = noise[:, 128:256]
    nimg[x] = nimg_w[...]
    last = []
    for d in range(1, 4):
        tx = (x + d) % NX
        last.append(go(remote(nimg.at[x], nimg.at[x], fs.at[d], fr.at[d], tx, y, z, c)))
    for copy in last:
        copy.wait_recv()
    noise_img = nimg[...].reshape(64, 128)
    clean = (noisy_ref[...].astype(F32) - jnp.sqrt(1.0 - signal_now) * noise_img) / jnp.sqrt(signal_now)
    out_ref[0] = (
        jnp.sqrt(signal_next) * clean + jnp.sqrt(1.0 - signal_next) * noise_img).astype(BF16)
    blank = jnp.zeros((1, 128), F32)
    above = jnp.concatenate([blank, clean[:-1]], axis=0)
    below = jnp.concatenate([clean[1:], blank], axis=0)
    no_row = jnp.full((1, 1), -1.0, F32)
    above_ok = jnp.concatenate([no_row, row_lat[:-1]], axis=0) == row_lat
    below_ok = jnp.concatenate([row_lat[1:], no_row], axis=0) == row_lat
    preview = (
        jnp.where(above_ok, exact_dot(above, band_s[0]), 0.0)
        + exact_dot(clean, band_s[1])
        + jnp.where(below_ok, exact_dot(below, band_s[2]), 0.0)
    )
    out_ref[1] = preview.astype(BF16)

    for copy in sent:
        copy.wait_send()

    @pl.when(c != own_core)
    def _():
        line_weight(0, 0).wait_send()
        weight_x(from_left, block_l, 0, 80, 4, right).wait_send()
        weight_x(from_right, block_r, 80, 64, 5, left).wait_send()

    @pl.when(owner)
    def _():
        weight_x(is_b, block_id, 0, 80, 0, right).wait_send()
        weight_x(is_b, block_id, 80, 64, 2, left).wait_send()
        weight_x(is_b, block_id, 80, 64, 1, right).wait_send()
        weight_x(is_b, block_id, 0, 80, 3, left).wait_send()


def shards(
    hidden, noisy_latent, tile_latent, timesteps, step_embedding, alpha_now, alpha_next,
    modulation, attention_in, attention_out, expand_weight, reduce_weight, noise_head, preview_kernel,
):
    vmem = pl.BlockSpec(memory_space=pltpu.VMEM)
    dma = pltpu.SemaphoreType.DMA
    out = pl.pallas_call(
        kernel,
        out_shape=jax.ShapeDtypeStruct((2, 64, 128), BF16),
        in_specs=[vmem] * 7 + [pl.BlockSpec(memory_space=pl.ANY)] * 2 + [vmem] * 5,
        out_specs=vmem,
        scratch_shapes=[
            pltpu.VMEM((8, 16, COLS), BF16),
            pltpu.VMEM((16, 768), BF16),
            pltpu.VMEM((8, 16, COLS), BF16),
            pltpu.VMEM((8, 32, COLS), BF16),
            pltpu.VMEM((8, 32, COLS), BF16),
            pltpu.VMEM((8, 8, COLS), F32),
            pltpu.VMEM((8, 8, COLS), F32),
            pltpu.VMEM((2, 16, COLS), F32),
            pltpu.VMEM((4, 2, 16, COLS), F32),
            pltpu.VMEM((16, D), F32),
            pltpu.VMEM((4, 16, COLS), BF16),
            pltpu.VMEM((256, 128), BF16),
            pltpu.VMEM((4, COLS, 4 * TILE), BF16),
            pltpu.VMEM((D, 4 * TILE), F32),
            pltpu.VMEM((D, 4 * TILE), BF16),
            pltpu.VMEM((16, 16, 768), BF16),
            pltpu.VMEM((2, 8, BLOCK, D), BF16),
            pltpu.VMEM((3, COLS, D), BF16),
            pltpu.VMEM((4, 2, BLOCK, D), BF16),
            pltpu.VMEM((D, D), BF16),
            pltpu.VMEM((3 * COLS, 4 * TILE), BF16),
            pltpu.VMEM((HEADS_HERE, 4 * TILE, HEAD_DIM), BF16),
            pltpu.VMEM((COLS, TILE), F32),
            pltpu.VMEM((4, 1, 128), F32),
            pltpu.VMEM((3, COLS, TILE), BF16),
            pltpu.VMEM((4, COLS, TILE), BF16),
            pltpu.VMEM((TILE, D), BF16),
            pltpu.VMEM((TILE, D), BF16),
            pltpu.VMEM((2, TILE, D), BF16),
            pltpu.VMEM((2, TILE, D), F32),
            pltpu.VMEM((TILE, D), F32),
            pltpu.VMEM((4, 16, 128), F32),
            pltpu.VMEM((16, 128), F32),
            pltpu.VMEM((3, 128, 128), F32),
            dma((8,)), dma((8,)),
            dma((8,)), dma((8,)),
            dma((8,)), dma((8,)),
            dma((8,)), dma((8,)),
            dma((4,)), dma((4,)),
            dma((2,)),
            dma((6,)), dma((6,)),
            dma((8,)), dma((16,)),
            dma((6,)), dma((6,)),
            dma((64,)), dma((64,)),
            dma((9,)), dma((9,)),
            dma((3,)), dma((3,)),
            dma((2,)), dma((2,)),
            dma((4,)), dma((4,)),
        ],
        compiler_params=pltpu.CompilerParams(
            collective_id=0, has_side_effects=True, vmem_limit_bytes=60 * 1024 * 1024),
        name="dit_block",
    )(
        hidden.T, modulation, reduce_weight.T, expand_weight, step_embedding,
        tile_latent[None, :], timesteps[None, :], attention_in.transpose(1, 2, 0), attention_out.reshape(2, BLOCK, D),
        noise_head.T, noisy_latent, alpha_now[None, :], alpha_next[None, :], preview_kernel,
    )
    return (out[0], out[1])


def solution(mesh):
    return jax.shard_map(
        shards,
        mesh=mesh,
        in_specs=(
            P("row", "col"),
            P("row", None),
            P(),
            P(),
            P(),
            P(),
            P(),
            P("row", None, "col"),
            P(None, None, "col"),
            P("col", None),
            P("row", "col"),
            P("col", "row"),
            P("col", None),
            P(),
        ),
        out_specs=(P("row", None), P("row", None)),
        check_vma=False,
    )
```

```python
import functools

import jax
import jax.numpy as jnp
from jax import lax
from jax.experimental import pallas as pl
from jax.experimental.pallas import tpu as pltpu
from jax.sharding import PartitionSpec as P

D = 1152
HEAD_DIM = 72
HEADS_HERE = 4
GRIDW = 16
STEPS = 50
TILE = 128
NX, NY, NZ = 4, 8, 8
COLS = D // NX
UNITS = 2304 // NX
ROWS = 9
BLOCK = 144
EPS_NORM = 1e-06
MESH = pl.DeviceIdType.MESH
F32 = jnp.float32
BF16 = jnp.bfloat16
CHUNKS = ((0, 48), (48, 32), (80, 32), (112, 32))


def swap_column(first, count):
    index = (iota((count, 1), 0) + first).astype(F32)
    major = jnp.floor((index + 0.5) * (1.0 / 144.0))
    rest = index - major * 144.0
    minor = jnp.floor((rest + 0.5) * (1.0 / 18.0))
    return minor * 144.0 + major * 18.0 + (rest - minor * 18.0)


def iota(shape, dim):
    return lax.broadcasted_iota(jnp.int32, shape, dim)


def dot(a, b):
    return jnp.dot(a, b, preferred_element_type=F32)


def dot_nt(a, b):
    return lax.dot_general(a, b, (((1,), (1,)), ((), ())), preferred_element_type=F32)


def dot_tn(a, b):
    return lax.dot_general(a, b, (((0,), (0,)), ((), ())), preferred_element_type=F32)


def exact_dot(a, b):
    return jnp.dot(a, b, preferred_element_type=F32, precision=lax.Precision.HIGHEST)


def normalized(values):
    mean_value = jnp.sum(values, axis=1, keepdims=True) / D
    spread = jnp.sum(values * values, axis=1, keepdims=True) / D - mean_value * mean_value
    return (values - mean_value) * lax.rsqrt(spread + EPS_NORM)


def kernel(
    hid_ref, mod_ref, red_ref, exp_ref, emb_ref, tl_ref, ts_ref, win_ref, wout_ref, nh_ref,
    noisy_ref, now_ref, next_ref, kern_ref,
    out_ref,
    mod_s, wp_s, mrecv, psend, precv, asend, arecv, adp_s, adp, adf, nh_s, rows_s, hall, norm_s, nin, w1, w_all,
    win_s, wout_s, swap_s, qkv, keys_s, att_s, lat_s, rsend, rrecv, hid_s, resid_s, nmx, osend, orecv,
    nimg, nimg_w, band_s,
    p1s, p1r, p2s, p2r, p4s, p4r, p5s, p5r, nhs, nhr, los, hs, hr, s1s, s1r, s3s, s3r, s4s, s4r,
    wxs, wxr, rss, rsr, exs, exr, fs, fr,
):
    r = lax.axis_index("row")
    x = lax.axis_index("col")
    y, z, c = r // (NZ * 2), (r // 2) % NZ, r % 2
    right, left = (x + 1) % NX, (x + 3) % NX

    def remote(src, dst, ss, rs, tx, ty, tz, tc):
        return pltpu.make_async_remote_copy(
            src_ref=src, dst_ref=dst, send_sem=ss, recv_sem=rs,
            device_id={"row": (ty * NZ + tz) * 2 + tc, "col": tx}, device_id_type=MESH,
        )

    sent = []

    def go(copy):
        copy.start()
        sent.append(copy)
        return copy

    win_load = pltpu.make_async_copy(win_ref, win_s, los.at[0])
    wout_load = pltpu.make_async_copy(wout_ref, wout_s.at[x], los.at[1])
    win_load.start()
    wout_load.start()
    barrier = pltpu.get_barrier_semaphore()

    def greet(tx, ty, tz, tc):
        pl.semaphore_signal(
            barrier, inc=1, device_id={"row": (ty * NZ + tz) * 2 + tc, "col": tx}, device_id_type=MESH
        )

    for d in range(8):
        for f in range(2):
            if d or f:
                greet(x, y, (z + d) % NZ, (c + f) % 2)
            if d:
                greet(x, (y + d) % NY, z, (c + f) % 2)
    for d in range(1, 4):
        for f in range(2):
            greet((x + d) % NX, y, z, (c + f) % 2)
    slab = (iota((128, 72), 0) % 16) * 8 + iota((128, 72), 0) // 16
    slab = jnp.where(iota((128, 72), 0) % 16 < ROWS, slab, -1)
    pick_mod = (slab == iota((128, 72), 1)).astype(F32).astype(BF16)
    mod_rows = mod_ref[...].astype(F32).reshape(72, COLS).astype(BF16)
    mod_s[...] = dot(pick_mod, mod_rows).astype(BF16).reshape(8, 16, COLS)
    pack = jnp.concatenate([red_ref[...].astype(F32), exp_ref[...].astype(F32)], axis=1)
    spare = jnp.concatenate([pack[7:9, 768:D], jnp.zeros((5, 384), F32)], axis=0)
    spare = jnp.concatenate([pack[0:7, 768:D], spare], axis=1)
    wp_s[...] = jnp.concatenate([pack[:, 0:768], spare], axis=0).astype(BF16)
    pl.semaphore_wait(barrier, 35)

    line_mod = []
    for d in range(1, 8):
        tz = (z + d) % NZ
        line_mod.append(go(remote(mod_s.at[tz], mrecv.at[z], p1s.at[d], p1r.at[d], x, y, tz, c)))
    mrecv[z] = mod_s[z]

    def hidden_copy(block, first, sem, tx):
        rows = pl.ds(first, 144)
        src = hid_ref.at[rows] if block is x else hall.at[block, rows]
        return remote(src, hall.at[block, rows], hs.at[sem], hr.at[sem], tx, y, z, c)

    h_r0 = go(hidden_copy(x, 0, 0, right))
    h_l1 = go(hidden_copy(x, 144, 2, left))
    h_r1 = go(hidden_copy(x, 144, 1, right))
    h_l0 = go(hidden_copy(x, 0, 3, left))
    hall[x] = hid_ref[...]
    heads = []
    for d in range(1, 4):
        heads.append(go(remote(nh_ref, nh_s.at[x], nhs.at[d], nhr.at[d], (x + d) % NX, y, z, c)))
    nh_s[x] = nh_ref[...]

    own_core = x % 2
    is_b = x // 2
    spot = z * (1 - is_b) + y * is_b
    block_id = y * (1 - is_b) + z * is_b
    owner = c == own_core

    def line_weight(d, sem):
        return remote(
            wp_s, w1.at[spot * 2 + c], s1s.at[d], s1r.at[sem],
            x, (y + d * is_b) % NY, (z + d * (1 - is_b)) % NZ, own_core)

    for d in range(1, 8):
        go(line_weight(d, d * 2 + c))

    @pl.when(c != own_core)
    def _():
        line_weight(0, 0).start()

    @pl.when(owner)
    def _():
        w1[spot * 2 + c] = wp_s[...]

    tile_lat = tl_ref[...].astype(F32)
    lat_steps = ts_ref[...].astype(F32)

    def looked_up(where_to, values):
        return jnp.sum(jnp.where(where_to, values, 0.0), axis=1, keepdims=True)

    table = emb_ref[...].astype(F32)
    table = (table / (1.0 + jnp.exp(-table))).astype(BF16)
    slot_col = iota((D, 128), 1)
    from_row = jnp.where(
        slot_col % 16 < ROWS, y * BLOCK + ((slot_col // 16) * 2 + c) * ROWS + slot_col % 16, -1)
    table = dot(table, (iota((D, 128), 0) == from_row).astype(F32).astype(BF16)).astype(BF16)
    slot = iota((256, 512), 0)
    slot_tile = (slot // 2) * 4 + 3 * (slot % 2)
    lane512 = iota((256, 512), 1)
    slot_lat = looked_up(slot_tile == lane512, tile_lat)
    slot_steps = looked_up(slot_lat == lane512.astype(F32), lat_steps)
    slot_hot = (slot_steps == iota((256, STEPS), 1).astype(F32)).astype(F32).astype(BF16)
    rows_s[...] = dot(slot_hot, table).astype(BF16)
    row_lat = looked_up(iota((64, 512), 1) == r * 4 + iota((64, 512), 0) // 16, tile_lat)
    for t in range(4):
        lat_s[t] = jnp.broadcast_to(row_lat[16 * t:16 * t + 1, :], (1, 128))

    for copy in line_mod:
        copy.wait_recv()
    part = dot(rows_s[...], mrecv[...].reshape(128, COLS))
    psend[...] = part.astype(BF16).reshape(8, 32, COLS)
    line_part = []
    for d in range(1, 8):
        ty = (y + d) % NY
        line_part.append(go(remote(psend.at[ty], precv.at[y], p2s.at[d], p2r.at[d], x, ty, z, c)))
    precv[y] = psend[y]

    h_r0.wait_recv()
    h_fr = go(hidden_copy(left, 0, 4, right))
    h_l1.wait_recv()
    h_fl = go(hidden_copy(right, 144, 5, left))

    def ring_copy(g, way, t, k):
        p = y * (1 - g) + z * g
        step = 1 if way == 0 else 7
        block = (p + t * (8 - step)) % 8
        first, count = CHUNKS[k]
        place = w_all.at[g, block, pl.ds(first, count)]
        sem = ((g * 2 + way) * 4 + t) * 4 + k
        return remote(
            place, place, s4s.at[sem], s4r.at[sem],
            x, (y + step * (1 - g)) % NY, (z + step * g) % NZ, c)

    def ring_chunks(way, t):
        if way == 0:
            return (0, 1, 2, 3) if t < 3 else (0, 1)
        return (2, 3, 0, 1) if t < 3 else (2, 3)

    def ring_start(g):
        for slot in range(4):
            for way in range(2):
                ring_copy(g, way, 0, ring_chunks(way, 0)[slot]).start()

    def weight_x(shard, block, first, count, sem, tx):
        place = w_all.at[shard, block, pl.ds(first, count)]
        return remote(place, place, s3s.at[sem], s3r.at[sem], tx, y, z, c)

    @pl.when(owner)
    def _():
        for d in range(1, 8):
            for k in range(2):
                line_weight(d, d * 2 + k).wait_recv()
        line_weight(0, 0).wait_recv()
        keep_row = iota((BLOCK, 256), 0)
        keep_col = iota((BLOCK, 256), 1)
        source = jnp.zeros((BLOCK, 256), jnp.int32)
        for k in range(1, 16):
            source = source + jnp.where(keep_row >= k * ROWS, 16 - ROWS, 0)
        word = keep_row + source - jnp.where(source >= 0, (source // (16 - ROWS)) * 16, 0)
        source = source + keep_row

        def picked(offset, valid):
            hit = (keep_col == source + offset) & valid
            return jnp.where(hit, 1.0, 0.0).astype(BF16)

        lines = w1[...].reshape(256, 768)
        w_all[is_b, block_id, :, 0:768] = dot(picked(0, word >= 0), lines).astype(BF16)
        w_all[is_b, block_id, :, 768:D] = (
            dot(picked(ROWS, word < 7), lines[:, 0:384])
            + dot(picked(ROWS - 7, word >= 7), lines[:, 384:768])).astype(BF16)
        weight_x(is_b, block_id, 0, 80, 0, right).start()
        weight_x(is_b, block_id, 80, 64, 2, left).start()
        weight_x(is_b, block_id, 80, 64, 1, right).start()
        weight_x(is_b, block_id, 0, 80, 3, left).start()
        ring_start(is_b)

    spread_out = (iota((4, 128), 0) == iota((4, 128), 1) % 4).astype(F32)
    gather_in = (iota((128, 4), 1) == iota((128, 4), 0) % 4).astype(F32)
    pixel_gap = iota((128, 128), 0) // 4 - iota((128, 128), 1) // 4
    for k in range(3):
        band = jnp.zeros((128, 128), F32)
        for off in range(3):
            full = exact_dot(gather_in, exact_dot(kern_ref[k, off], spread_out))
            band = band + jnp.where(pixel_gap == off - 1, full, 0.0)
        band_s[k] = band

    for copy in line_part:
        copy.wait_recv()
    total = jnp.sum(precv[...].astype(F32), axis=0)
    asend[...] = jnp.zeros((8, 8, COLS), F32)
    for k in range(8):
        asend[k, 0:4, :] = total[4 * k:4 * k + 4, :]
    line_rows = []
    for d in range(1, 8):
        tz = (z + d) % NZ
        line_rows.append(go(remote(asend.at[tz], arecv.at[z], p4s.at[d], p4r.at[d], x, y, tz, c)))
    arecv[z] = asend[z]

    from_left = left // 2
    from_right = right // 2
    block_l = y * (1 - from_left) + z * from_left
    block_r = y * (1 - from_right) + z * from_right

    @pl.when(c != own_core)
    def _():
        weight_x(from_left, block_l, 0, 80, 0, right).wait_recv()
        weight_x(from_left, block_l, 0, 80, 4, right).start()
        weight_x(from_right, block_r, 80, 64, 2, left).wait_recv()
        weight_x(from_right, block_r, 80, 64, 5, left).start()
        weight_x(from_left, block_l, 80, 64, 1, right).wait_recv()
        weight_x(from_right, block_r, 0, 80, 3, left).wait_recv()
        ring_start(0)
        ring_start(1)

    other = 1 - is_b
    block_o = y * (1 - other) + z * other

    @pl.when(owner)
    def _():
        weight_x(other, block_o, 0, 80, 4, right).wait_recv()
        weight_x(other, block_o, 80, 64, 5, left).wait_recv()
        ring_start(other)

    ring = {}
    for g in range(2):
        for way in range(2):
            for k in ring_chunks(way, 0):
                ring[g, way, 0, k] = ring_copy(g, way, 0, k)
                sent.append(ring[g, way, 0, k])
    pending = []
    for t in range(1, 4):
        for slot in range(len(ring_chunks(0, t))):
            for g in range(2):
                for way in range(2):
                    pending.append((g, way, t, ring_chunks(way, t)[slot]))
    waited = set()

    def pump(count):
        for _ in range(min(count, len(pending))):
            g, way, t, k = pending.pop(0)
            ring[g, way, t - 1, k].wait_recv()
            waited.add((g, way, t - 1, k))
            ring[g, way, t, k] = go(ring_copy(g, way, t, k))

    h_r1.wait_recv()
    h_l0.wait_recv()
    h_fr.wait_recv()
    h_fl.wait_recv()
    for t in range(4):
        values = hall[:, :, t * TILE:(t + 1) * TILE].reshape(D, TILE).astype(F32)
        mean_value = jnp.sum(values, axis=0, keepdims=True) / D
        spread = jnp.sum(values * values, axis=0, keepdims=True) / D - mean_value * mean_value
        norm_s[:, t * TILE:(t + 1) * TILE] = (values - mean_value) * lax.rsqrt(spread + EPS_NORM)

    for copy in line_rows:
        copy.wait_recv()
    for k in range(8):
        for f in range(2):
            adp_s[f, 2 * k:2 * k + 2, :] = arecv[k, 2 * f:2 * f + 2, :]
    cross = []
    for d in range(4):
        for f in range(2):
            if d or f:
                tc = (c + f) % 2
                cross.append(go(remote(
                    adp_s.at[tc], adp.at[x, c], p5s.at[d * 2 + f], p5r.at[d * 2 + f],
                    (x + d) % NX, y, z, tc)))
    adp[x, c] = adp_s[c]
    def wout_x(shard, first, count, sem, tx):
        place = wout_s.at[shard, c, pl.ds(first, count)]
        return remote(place, place, wxs.at[sem], wxr.at[sem], tx, y, z, c)

    wout_load.wait()
    o_r0 = go(wout_x(x, 0, 80, 0, right))
    o_l1 = go(wout_x(x, 80, 64, 2, left))
    o_r1 = go(wout_x(x, 80, 64, 1, right))
    o_l0 = go(wout_x(x, 0, 80, 3, left))

    pump(8)

    for copy in cross:
        copy.wait_recv()
    for k in range(4):
        adf[:, k * COLS:(k + 1) * COLS] = adp[k, 0] + adp[k, 1]

    def rows_of(tile, which):
        later = (lat_s[tile, :, 0:1] == lat_s[3, :, 0:1]).astype(F32)
        return later * adf[2 * which + 1:2 * which + 2, :] + (1.0 - later) * adf[2 * which:2 * which + 1, :]

    columns = jnp.concatenate([rows_of(t, k) for k in (0, 1) for t in range(4)], axis=0).T
    for t in range(4):
        values = norm_s[:, t * TILE:(t + 1) * TILE]
        nin[:, t * TILE:(t + 1) * TILE] = (
            values * (1.0 + columns[:, 4 + t:5 + t]) + columns[:, t:t + 1]).astype(BF16)
        pump(4)
    o_r0.wait_recv()
    o_fr = go(wout_x(left, 0, 80, 4, right))
    o_l1.wait_recv()
    o_fl = go(wout_x(right, 80, 64, 5, left))
    win_load.wait()
    win = win_s[...].reshape(3 * COLS, D)
    for t in range(2):
        lanes = slice(t * 256, (t + 1) * 256)
        qkv[:, lanes] = dot(win, nin[:, lanes]).astype(BF16)
    pump(6)
    for h in range(HEADS_HERE):
        rows = slice(COLS + h * HEAD_DIM, COLS + (h + 1) * HEAD_DIM)
        keys_s[h] = qkv[rows, :].T

    scale_factor = HEAD_DIM ** (-0.5)

    def attend(tile):
        lanes = pl.ds(pl.multiple_of(tile * TILE, TILE), TILE)
        bias = [
            jnp.where(lat_s[u] == lat_s[tile], 0.0, -1e30) for u in range(4)]
        for h in range(HEADS_HERE):
            rows = slice(h * HEAD_DIM, (h + 1) * HEAD_DIM)
            query = qkv[rows, lanes]
            mates = qkv[2 * COLS + rows.start:2 * COLS + rows.stop, :]
            scores = dot(keys_s[h], query) * scale_factor
            scores = jnp.concatenate(
                [scores[u * TILE:(u + 1) * TILE] + bias[u] for u in range(4)], axis=0)
            raised = jnp.exp(scores - jnp.max(scores, axis=0, keepdims=True))
            share = 1.0 / jnp.sum(raised, axis=0, keepdims=True)
            att_s[rows, :] = dot(mates, raised.astype(BF16)) * share
        return att_s[...].astype(BF16)

    facing = (x + 2) % NX
    share_out = []
    for k, tile in enumerate((facing, right, left)):
        rsend[k] = attend(tile)
        share_out.append(go(remote(rsend.at[k], rrecv.at[x], rss.at[k], rsr.at[k], tile, y, z, c)))
        pump(4)
    rrecv[x] = attend(x)
    def wout_core(shard, sem):
        place = wout_s.at[shard, c]
        return remote(place, place, wxs.at[sem], wxr.at[sem], x, y, z, 1 - c)

    o_r1.wait_recv()
    o_cl = go(wout_core(left, 6))
    o_l0.wait_recv()
    o_cr = go(wout_core(right, 7))
    o_fr.wait_recv()
    o_fl.wait_recv()
    o_co = go(wout_core(facing, 8))
    pump(8)
    hid_s[...] = hall[:, :, pl.ds(pl.multiple_of(x * TILE, TILE), TILE)].reshape(D, TILE).astype(F32).T.astype(BF16)

    for k in range(9):
        rows = slice(k * 128, (k + 1) * 128)
        swap_s[rows, :] = (swap_column(k * 128, 128) == iota((128, D), 1).astype(F32)).astype(F32).astype(BF16)
    for copy in share_out:
        copy.wait_recv()
    o_cl.wait_recv()
    o_cr.wait_recv()
    o_co.wait_recv()
    attn_sum = dot_tn(rrecv[...].reshape(D, TILE), wout_s[...].reshape(D, D))
    residual = (hid_s[...].astype(F32) + rows_of(x, 2) * attn_sum).astype(BF16)
    resid_s[...] = residual
    values = normalized(residual.astype(F32))
    nmx[c] = (values * (1.0 + rows_of(x, 4)) + rows_of(x, 3)).astype(BF16)
    swap_mid = go(remote(nmx.at[c], nmx.at[c], exs.at[0], exr.at[0], x, y, z, 1 - c))
    pump(len(pending))
    swap_mid.wait_recv()
    both = nmx[...].reshape(256, D)
    for key, copy in ring.items():
        if key not in waited:
            copy.wait_recv()
    both_swapped = dot(both, swap_s[...]).astype(BF16)

    def mlp(g, features):
        packed = w_all.at[g]
        expanded = dot(features, packed[:, :, 512:D].reshape(D, D - 512))[:, 64:64 + UNITS]
        activated = jax.nn.gelu(expanded, approximate=True).astype(BF16)
        return dot_nt(activated, packed[:, :, 0:UNITS].reshape(D, UNITS)).astype(BF16)

    mlp_part = mlp(0, both).astype(F32) + dot(mlp(1, both_swapped), swap_s[...])
    osend[...] = mlp_part.reshape(2, TILE, D)
    swap_out = go(remote(osend.at[1 - c], orecv, exs.at[1], exr.at[1], x, y, z, 1 - c))

    row_steps = looked_up(row_lat == iota((64, 512), 1).astype(F32), lat_steps)
    row_hot = row_steps == iota((64, STEPS), 1).astype(F32)
    signal_now = looked_up(row_hot, now_ref[...])
    signal_next = looked_up(row_hot, next_ref[...])
    for copy in heads:
        copy.wait_recv()
    head = jnp.concatenate([nh_s[k].astype(F32) for k in range(4)], axis=1)
    head_rows = jnp.concatenate([head[0:8, :]] * 16 + [head[8:16, :]] * 16, axis=0).astype(BF16)

    swap_out.wait_recv()
    mlp_sum = osend[c] + orecv[...]
    second = (resid_s[...].astype(F32) + rows_of(x, 5) * mlp_sum).astype(BF16)
    values = normalized(second.astype(F32))
    normed_out = (values * (1.0 + rows_of(x, 7)) + rows_of(x, 6)).astype(BF16)
    noise = dot_nt(normed_out, head_rows)
    token_col = iota((TILE, 256), 0) % GRIDW
    lane_col = (iota((TILE, 256), 1) % 128) // 8
    noise = jnp.where(token_col == lane_col, noise, 0.0)
    noise = jnp.sum(noise.reshape(8, GRIDW, 256), axis=1)
    nimg_w[pl.ds(0, 8, 2), :] = noise[:, 0:128]
    nimg_w[pl.ds(1, 8, 2), :] = noise[:, 128:256]
    nimg[x] = nimg_w[...]
    last = []
    for d in range(1, 4):
        tx = (x + d) % NX
        last.append(go(remote(nimg.at[x], nimg.at[x], fs.at[d], fr.at[d], tx, y, z, c)))
    for copy in last:
        copy.wait_recv()
    noise_img = nimg[...].reshape(64, 128)
    clean = (noisy_ref[...].astype(F32) - jnp.sqrt(1.0 - signal_now) * noise_img) / jnp.sqrt(signal_now)
    out_ref[0] = (
        jnp.sqrt(signal_next) * clean + jnp.sqrt(1.0 - signal_next) * noise_img).astype(BF16)
    blank = jnp.zeros((1, 128), F32)
    above = jnp.concatenate([blank, clean[:-1]], axis=0)
    below = jnp.concatenate([clean[1:], blank], axis=0)
    no_row = jnp.full((1, 1), -1.0, F32)
    above_ok = jnp.concatenate([no_row, row_lat[:-1]], axis=0) == row_lat
    below_ok = jnp.concatenate([row_lat[1:], no_row], axis=0) == row_lat
    preview = (
        jnp.where(above_ok, exact_dot(above, band_s[0]), 0.0)
        + exact_dot(clean, band_s[1])
        + jnp.where(below_ok, exact_dot(below, band_s[2]), 0.0)
    )
    out_ref[1] = preview.astype(BF16)

    for copy in sent:
        copy.wait_send()

    @pl.when(c != own_core)
    def _():
        line_weight(0, 0).wait_send()
        weight_x(from_left, block_l, 0, 80, 4, right).wait_send()
        weight_x(from_right, block_r, 80, 64, 5, left).wait_send()

    @pl.when(owner)
    def _():
        weight_x(is_b, block_id, 0, 80, 0, right).wait_send()
        weight_x(is_b, block_id, 80, 64, 2, left).wait_send()
        weight_x(is_b, block_id, 80, 64, 1, right).wait_send()
        weight_x(is_b, block_id, 0, 80, 3, left).wait_send()


def shards(
    hidden, noisy_latent, tile_latent, timesteps, step_embedding, alpha_now, alpha_next,
    modulation, attention_in, attention_out, expand_weight, reduce_weight, noise_head, preview_kernel,
):
    vmem = pl.BlockSpec(memory_space=pltpu.VMEM)
    dma = pltpu.SemaphoreType.DMA
    out = pl.pallas_call(
        kernel,
        out_shape=jax.ShapeDtypeStruct((2, 64, 128), BF16),
        in_specs=[vmem] * 7 + [pl.BlockSpec(memory_space=pl.ANY)] * 2 + [vmem] * 5,
        out_specs=vmem,
        scratch_shapes=[
            pltpu.VMEM((8, 16, COLS), BF16),
            pltpu.VMEM((16, 768), BF16),
            pltpu.VMEM((8, 16, COLS), BF16),
            pltpu.VMEM((8, 32, COLS), BF16),
            pltpu.VMEM((8, 32, COLS), BF16),
            pltpu.VMEM((8, 8, COLS), F32),
            pltpu.VMEM((8, 8, COLS), F32),
            pltpu.VMEM((2, 16, COLS), F32),
            pltpu.VMEM((4, 2, 16, COLS), F32),
            pltpu.VMEM((16, D), F32),
            pltpu.VMEM((4, 16, COLS), BF16),
            pltpu.VMEM((256, 128), BF16),
            pltpu.VMEM((4, COLS, 4 * TILE), BF16),
            pltpu.VMEM((D, 4 * TILE), F32),
            pltpu.VMEM((D, 4 * TILE), BF16),
            pltpu.VMEM((16, 16, 768), BF16),
            pltpu.VMEM((2, 8, BLOCK, D), BF16),
            pltpu.VMEM((3, COLS, D), BF16),
            pltpu.VMEM((4, 2, BLOCK, D), BF16),
            pltpu.VMEM((D, D), BF16),
            pltpu.VMEM((3 * COLS, 4 * TILE), BF16),
            pltpu.VMEM((HEADS_HERE, 4 * TILE, HEAD_DIM), BF16),
            pltpu.VMEM((COLS, TILE), F32),
            pltpu.VMEM((4, 1, 128), F32),
            pltpu.VMEM((3, COLS, TILE), BF16),
            pltpu.VMEM((4, COLS, TILE), BF16),
            pltpu.VMEM((TILE, D), BF16),
            pltpu.VMEM((TILE, D), BF16),
            pltpu.VMEM((2, TILE, D), BF16),
            pltpu.VMEM((2, TILE, D), F32),
            pltpu.VMEM((TILE, D), F32),
            pltpu.VMEM((4, 16, 128), F32),
            pltpu.VMEM((16, 128), F32),
            pltpu.VMEM((3, 128, 128), F32),
            dma((8,)), dma((8,)),
            dma((8,)), dma((8,)),
            dma((8,)), dma((8,)),
            dma((8,)), dma((8,)),
            dma((4,)), dma((4,)),
            dma((2,)),
            dma((6,)), dma((6,)),
            dma((8,)), dma((16,)),
            dma((6,)), dma((6,)),
            dma((64,)), dma((64,)),
            dma((9,)), dma((9,)),
            dma((3,)), dma((3,)),
            dma((2,)), dma((2,)),
            dma((4,)), dma((4,)),
        ],
        compiler_params=pltpu.CompilerParams(
            collective_id=0, has_side_effects=True, vmem_limit_bytes=60 * 1024 * 1024),
        name="dit_block",
    )(
        hidden.T, modulation, reduce_weight.T, expand_weight, step_embedding,
        tile_latent[None, :], timesteps[None, :], attention_in.transpose(1, 2, 0), attention_out.reshape(2, BLOCK, D),
        noise_head.T, noisy_latent, alpha_now[None, :], alpha_next[None, :], preview_kernel,
    )
    return (out[0], out[1])


def solution(mesh):
    return jax.shard_map(
        shards,
        mesh=mesh,
        in_specs=(
            P("row", "col"),
            P("row", None),
            P(),
            P(),
            P(),
            P(),
            P(),
            P("row", None, "col"),
            P(None, None, "col"),
            P("col", None),
            P("row", "col"),
            P("col", "row"),
            P("col", None),
            P(),
        ),
        out_specs=(P("row", None), P("row", None)),
        check_vma=False,
    )
```

```python
import functools

import jax
import jax.numpy as jnp
from jax import lax
from jax.experimental import pallas as pl
from jax.experimental.pallas import tpu as pltpu
from jax.sharding import PartitionSpec as P

D = 1152
HEAD_DIM = 72
HEADS_HERE = 4
GRIDW = 16
STEPS = 50
TILE = 128
NX, NY, NZ = 4, 8, 8
COLS = D // NX
UNITS = 2304 // NX
ROWS = 9
BLOCK = 144
EPS_NORM = 1e-06
MESH = pl.DeviceIdType.MESH
F32 = jnp.float32
BF16 = jnp.bfloat16
CHUNKS = ((0, 48), (48, 32), (80, 32), (112, 32))


def swap_column(first, count):
    index = (iota((count, 1), 0) + first).astype(F32)
    major = jnp.floor((index + 0.5) * (1.0 / 144.0))
    rest = index - major * 144.0
    minor = jnp.floor((rest + 0.5) * (1.0 / 18.0))
    return minor * 144.0 + major * 18.0 + (rest - minor * 18.0)


def iota(shape, dim):
    return lax.broadcasted_iota(jnp.int32, shape, dim)


def dot(a, b):
    return jnp.dot(a, b, preferred_element_type=F32)


def dot_nt(a, b):
    return lax.dot_general(a, b, (((1,), (1,)), ((), ())), preferred_element_type=F32)


def dot_tn(a, b):
    return lax.dot_general(a, b, (((0,), (0,)), ((), ())), preferred_element_type=F32)


def exact_dot(a, b):
    return jnp.dot(a, b, preferred_element_type=F32, precision=lax.Precision.HIGHEST)


def normalized(values):
    mean_value = jnp.sum(values, axis=1, keepdims=True) / D
    spread = jnp.sum(values * values, axis=1, keepdims=True) / D - mean_value * mean_value
    return (values - mean_value) * lax.rsqrt(spread + EPS_NORM)


def kernel(
    hid_ref, mod_ref, red_ref, exp_ref, emb_ref, tl_ref, ts_ref, win_ref, wout_ref, nh_ref,
    noisy_ref, now_ref, next_ref, kern_ref,
    out_ref,
    mod_s, wp_s, mrecv, psend, precv, asend, arecv, adp_s, adp, adf, nh_s, rows_s, hall, norm_s, nin, w1, w_all,
    win_s, wout_s, swap_s, qkv, keys_s, att_s, lat_s, rsend, rrecv, hid_s, resid_s, nmx, osend, orecv,
    nimg, nimg_w, band_s,
    p1s, p1r, p2s, p2r, p4s, p4r, p5s, p5r, nhs, nhr, los, hs, hr, s1s, s1r, s3s, s3r, s4s, s4r,
    wxs, wxr, rss, rsr, exs, exr, fs, fr,
):
    r = lax.axis_index("row")
    x = lax.axis_index("col")
    y, z, c = r // (NZ * 2), (r // 2) % NZ, r % 2
    right, left = (x + 1) % NX, (x + 3) % NX

    def remote(src, dst, ss, rs, tx, ty, tz, tc):
        return pltpu.make_async_remote_copy(
            src_ref=src, dst_ref=dst, send_sem=ss, recv_sem=rs,
            device_id={"row": (ty * NZ + tz) * 2 + tc, "col": tx}, device_id_type=MESH,
        )

    sent = []

    def go(copy):
        copy.start()
        sent.append(copy)
        return copy

    win_load = pltpu.make_async_copy(win_ref, win_s, los.at[0])
    wout_load = pltpu.make_async_copy(wout_ref, wout_s.at[x], los.at[1])
    win_load.start()
    wout_load.start()
    barrier = pltpu.get_barrier_semaphore()

    def greet(tx, ty, tz, tc):
        pl.semaphore_signal(
            barrier, inc=1, device_id={"row": (ty * NZ + tz) * 2 + tc, "col": tx}, device_id_type=MESH
        )

    for d in range(8):
        for f in range(2):
            if d or f:
                greet(x, y, (z + d) % NZ, (c + f) % 2)
            if d:
                greet(x, (y + d) % NY, z, (c + f) % 2)
    for d in range(1, 4):
        for f in range(2):
            greet((x + d) % NX, y, z, (c + f) % 2)
    slab = (iota((128, 72), 0) % 16) * 8 + iota((128, 72), 0) // 16
    slab = jnp.where(iota((128, 72), 0) % 16 < ROWS, slab, -1)
    pick_mod = (slab == iota((128, 72), 1)).astype(F32).astype(BF16)
    mod_rows = mod_ref[...].astype(F32).reshape(72, COLS).astype(BF16)
    mod_s[...] = dot(pick_mod, mod_rows).astype(BF16).reshape(8, 16, COLS)
    pack = jnp.concatenate([red_ref[...].astype(F32), exp_ref[...].astype(F32)], axis=1)
    spare = jnp.concatenate([pack[7:9, 768:D], jnp.zeros((5, 384), F32)], axis=0)
    spare = jnp.concatenate([pack[0:7, 768:D], spare], axis=1)
    wp_s[...] = jnp.concatenate([pack[:, 0:768], spare], axis=0).astype(BF16)
    pl.semaphore_wait(barrier, 35)

    line_mod = []
    for d in range(1, 8):
        tz = (z + d) % NZ
        line_mod.append(go(remote(mod_s.at[tz], mrecv.at[z], p1s.at[d], p1r.at[d], x, y, tz, c)))
    mrecv[z] = mod_s[z]

    def hidden_copy(block, first, sem, tx):
        rows = pl.ds(first, 144)
        src = hid_ref.at[rows] if block is x else hall.at[block, rows]
        return remote(src, hall.at[block, rows], hs.at[sem], hr.at[sem], tx, y, z, c)

    h_r0 = go(hidden_copy(x, 0, 0, right))
    h_l1 = go(hidden_copy(x, 144, 2, left))
    h_r1 = go(hidden_copy(x, 144, 1, right))
    h_l0 = go(hidden_copy(x, 0, 3, left))
    hall[x] = hid_ref[...]
    heads = []
    for d in range(1, 4):
        heads.append(go(remote(nh_ref, nh_s.at[x], nhs.at[d], nhr.at[d], (x + d) % NX, y, z, c)))
    nh_s[x] = nh_ref[...]

    own_core = x % 2
    is_b = x // 2
    spot = z * (1 - is_b) + y * is_b
    block_id = y * (1 - is_b) + z * is_b
    owner = c == own_core

    def line_weight(d, sem):
        return remote(
            wp_s, w1.at[spot * 2 + c], s1s.at[d], s1r.at[sem],
            x, (y + d * is_b) % NY, (z + d * (1 - is_b)) % NZ, own_core)

    for d in range(1, 8):
        go(line_weight(d, d * 2 + c))

    @pl.when(c != own_core)
    def _():
        line_weight(0, 0).start()

    @pl.when(owner)
    def _():
        w1[spot * 2 + c] = wp_s[...]

    tile_lat = tl_ref[...].astype(F32)
    lat_steps = ts_ref[...].astype(F32)

    def looked_up(where_to, values):
        return jnp.sum(jnp.where(where_to, values, 0.0), axis=1, keepdims=True)

    table = emb_ref[...].astype(F32)
    table = (table / (1.0 + jnp.exp(-table))).astype(BF16)
    slot_col = iota((D, 128), 1)
    from_row = jnp.where(
        slot_col % 16 < ROWS, y * BLOCK + ((slot_col // 16) * 2 + c) * ROWS + slot_col % 16, -1)
    table = dot(table, (iota((D, 128), 0) == from_row).astype(F32).astype(BF16)).astype(BF16)
    slot = iota((256, 512), 0)
    slot_tile = (slot // 2) * 4 + 3 * (slot % 2)
    lane512 = iota((256, 512), 1)
    slot_lat = looked_up(slot_tile == lane512, tile_lat)
    slot_steps = looked_up(slot_lat == lane512.astype(F32), lat_steps)
    slot_hot = (slot_steps == iota((256, STEPS), 1).astype(F32)).astype(F32).astype(BF16)
    rows_s[...] = dot(slot_hot, table).astype(BF16)
    row_lat = looked_up(iota((64, 512), 1) == r * 4 + iota((64, 512), 0) // 16, tile_lat)
    for t in range(4):
        lat_s[t] = jnp.broadcast_to(row_lat[16 * t:16 * t + 1, :], (1, 128))

    for copy in line_mod:
        copy.wait_recv()
    part = dot(rows_s[...], mrecv[...].reshape(128, COLS))
    psend[...] = part.astype(BF16).reshape(8, 32, COLS)
    line_part = []
    for d in range(1, 8):
        ty = (y + d) % NY
        line_part.append(go(remote(psend.at[ty], precv.at[y], p2s.at[d], p2r.at[d], x, ty, z, c)))
    precv[y] = psend[y]

    h_r0.wait_recv()
    h_fr = go(hidden_copy(left, 0, 4, right))
    h_l1.wait_recv()
    h_fl = go(hidden_copy(right, 144, 5, left))

    def ring_copy(g, way, t, k):
        p = y * (1 - g) + z * g
        step = 1 if way == 0 else 7
        block = (p + t * (8 - step)) % 8
        first, count = CHUNKS[k]
        place = w_all.at[g, block, pl.ds(first, count)]
        sem = ((g * 2 + way) * 4 + t) * 4 + k
        return remote(
            place, place, s4s.at[sem], s4r.at[sem],
            x, (y + step * (1 - g)) % NY, (z + step * g) % NZ, c)

    def ring_chunks(way, t):
        if way == 0:
            return (0, 1, 2, 3) if t < 3 else (0, 1)
        return (2, 3, 0, 1) if t < 3 else (2, 3)

    def ring_start(g):
        for slot in range(4):
            for way in range(2):
                ring_copy(g, way, 0, ring_chunks(way, 0)[slot]).start()

    def weight_x(shard, block, first, count, sem, tx):
        place = w_all.at[shard, block, pl.ds(first, count)]
        return remote(place, place, s3s.at[sem], s3r.at[sem], tx, y, z, c)

    @pl.when(owner)
    def _():
        for d in range(1, 8):
            for k in range(2):
                line_weight(d, d * 2 + k).wait_recv()
        line_weight(0, 0).wait_recv()
        keep_row = iota((BLOCK, 256), 0)
        keep_col = iota((BLOCK, 256), 1)
        source = jnp.zeros((BLOCK, 256), jnp.int32)
        for k in range(1, 16):
            source = source + jnp.where(keep_row >= k * ROWS, 16 - ROWS, 0)
        word = keep_row + source - jnp.where(source >= 0, (source // (16 - ROWS)) * 16, 0)
        source = source + keep_row

        def picked(offset, valid):
            hit = (keep_col == source + offset) & valid
            return jnp.where(hit, 1.0, 0.0).astype(BF16)

        lines = w1[...].reshape(256, 768)
        w_all[is_b, block_id, :, 0:768] = dot(picked(0, word >= 0), lines).astype(BF16)
        w_all[is_b, block_id, :, 768:D] = (
            dot(picked(ROWS, word < 7), lines[:, 0:384])
            + dot(picked(ROWS - 7, word >= 7), lines[:, 384:768])).astype(BF16)
        weight_x(is_b, block_id, 0, 80, 0, right).start()
        weight_x(is_b, block_id, 80, 64, 2, left).start()
        weight_x(is_b, block_id, 80, 64, 1, right).start()
        weight_x(is_b, block_id, 0, 80, 3, left).start()
        ring_start(is_b)

    spread_out = (iota((4, 128), 0) == iota((4, 128), 1) % 4).astype(F32)
    gather_in = (iota((128, 4), 1) == iota((128, 4), 0) % 4).astype(F32)
    pixel_gap = iota((128, 128), 0) // 4 - iota((128, 128), 1) // 4
    for k in range(3):
        band = jnp.zeros((128, 128), F32)
        for off in range(3):
            full = exact_dot(gather_in, exact_dot(kern_ref[k, off], spread_out))
            band = band + jnp.where(pixel_gap == off - 1, full, 0.0)
        band_s[k] = band

    for copy in line_part:
        copy.wait_recv()
    total = jnp.sum(precv[...].astype(F32), axis=0)
    asend[...] = jnp.zeros((8, 8, COLS), F32)
    for k in range(8):
        asend[k, 0:4, :] = total[4 * k:4 * k + 4, :]
    line_rows = []
    for d in range(1, 8):
        tz = (z + d) % NZ
        line_rows.append(go(remote(asend.at[tz], arecv.at[z], p4s.at[d], p4r.at[d], x, y, tz, c)))
    arecv[z] = asend[z]

    from_left = left // 2
    from_right = right // 2
    block_l = y * (1 - from_left) + z * from_left
    block_r = y * (1 - from_right) + z * from_right

    @pl.when(c != own_core)
    def _():
        weight_x(from_left, block_l, 0, 80, 0, right).wait_recv()
        weight_x(from_left, block_l, 0, 80, 4, right).start()
        weight_x(from_right, block_r, 80, 64, 2, left).wait_recv()
        weight_x(from_right, block_r, 80, 64, 5, left).start()
        weight_x(from_left, block_l, 80, 64, 1, right).wait_recv()
        weight_x(from_right, block_r, 0, 80, 3, left).wait_recv()
        ring_start(0)
        ring_start(1)

    other = 1 - is_b
    block_o = y * (1 - other) + z * other

    @pl.when(owner)
    def _():
        weight_x(other, block_o, 0, 80, 4, right).wait_recv()
        weight_x(other, block_o, 80, 64, 5, left).wait_recv()
        ring_start(other)

    ring = {}
    for g in range(2):
        for way in range(2):
            for k in ring_chunks(way, 0):
                ring[g, way, 0, k] = ring_copy(g, way, 0, k)
                sent.append(ring[g, way, 0, k])
    pending = []
    for t in range(1, 4):
        for slot in range(len(ring_chunks(0, t))):
            for g in range(2):
                for way in range(2):
                    pending.append((g, way, t, ring_chunks(way, t)[slot]))
    waited = set()

    def pump(count):
        for _ in range(min(count, len(pending))):
            g, way, t, k = pending.pop(0)
            ring[g, way, t - 1, k].wait_recv()
            waited.add((g, way, t - 1, k))
            ring[g, way, t, k] = go(ring_copy(g, way, t, k))

    h_r1.wait_recv()
    h_l0.wait_recv()
    h_fr.wait_recv()
    h_fl.wait_recv()
    for t in range(4):
        values = hall[:, :, t * TILE:(t + 1) * TILE].reshape(D, TILE).astype(F32)
        mean_value = jnp.sum(values, axis=0, keepdims=True) / D
        spread = jnp.sum(values * values, axis=0, keepdims=True) / D - mean_value * mean_value
        norm_s[:, t * TILE:(t + 1) * TILE] = (values - mean_value) * lax.rsqrt(spread + EPS_NORM)

    for copy in line_rows:
        copy.wait_recv()
    for k in range(8):
        for f in range(2):
            adp_s[f, 2 * k:2 * k + 2, :] = arecv[k, 2 * f:2 * f + 2, :]
    cross = []
    for d in range(4):
        for f in range(2):
            if d or f:
                tc = (c + f) % 2
                cross.append(go(remote(
                    adp_s.at[tc], adp.at[x, c], p5s.at[d * 2 + f], p5r.at[d * 2 + f],
                    (x + d) % NX, y, z, tc)))
    adp[x, c] = adp_s[c]
    def wout_x(shard, first, count, sem, tx):
        place = wout_s.at[shard, c, pl.ds(first, count)]
        return remote(place, place, wxs.at[sem], wxr.at[sem], tx, y, z, c)

    wout_load.wait()
    o_r0 = go(wout_x(x, 0, 80, 0, right))
    o_l1 = go(wout_x(x, 80, 64, 2, left))
    o_r1 = go(wout_x(x, 80, 64, 1, right))
    o_l0 = go(wout_x(x, 0, 80, 3, left))

    pump(8)

    for copy in cross:
        copy.wait_recv()
    for k in range(4):
        adf[:, k * COLS:(k + 1) * COLS] = adp[k, 0] + adp[k, 1]

    def rows_of(tile, which):
        later = (lat_s[tile, :, 0:1] == lat_s[3, :, 0:1]).astype(F32)
        return later * adf[2 * which + 1:2 * which + 2, :] + (1.0 - later) * adf[2 * which:2 * which + 1, :]

    columns = jnp.concatenate([rows_of(t, k) for k in (0, 1) for t in range(4)], axis=0).T
    for t in range(4):
        values = norm_s[:, t * TILE:(t + 1) * TILE]
        nin[:, t * TILE:(t + 1) * TILE] = (
            values * (1.0 + columns[:, 4 + t:5 + t]) + columns[:, t:t + 1]).astype(BF16)
        pump(4)
    o_r0.wait_recv()
    o_fr = go(wout_x(left, 0, 80, 4, right))
    o_l1.wait_recv()
    o_fl = go(wout_x(right, 80, 64, 5, left))
    win_load.wait()
    win = win_s[...].reshape(3 * COLS, D)
    for t in range(2):
        lanes = slice(t * 256, (t + 1) * 256)
        qkv[:, lanes] = dot(win, nin[:, lanes]).astype(BF16)
    pump(6)
    for h in range(HEADS_HERE):
        rows = slice(COLS + h * HEAD_DIM, COLS + (h + 1) * HEAD_DIM)
        keys_s[h] = qkv[rows, :].T

    scale_factor = HEAD_DIM ** (-0.5)

    def attend(tile):
        lanes = pl.ds(pl.multiple_of(tile * TILE, TILE), TILE)
        bias = [
            jnp.where(lat_s[u] == lat_s[tile], 0.0, -1e30) for u in range(4)]
        for h in range(HEADS_HERE):
            rows = slice(h * HEAD_DIM, (h + 1) * HEAD_DIM)
            query = qkv[rows, lanes]
            mates = qkv[2 * COLS + rows.start:2 * COLS + rows.stop, :]
            scores = dot(keys_s[h], query) * scale_factor
            scores = jnp.concatenate(
                [scores[u * TILE:(u + 1) * TILE] + bias[u] for u in range(4)], axis=0)
            raised = jnp.exp(scores - jnp.max(scores, axis=0, keepdims=True))
            share = 1.0 / jnp.sum(raised, axis=0, keepdims=True)
            att_s[rows, :] = dot(mates, raised.astype(BF16)) * share
        return att_s[...].astype(BF16)

    facing = (x + 2) % NX
    share_out = []
    for k, tile in enumerate((facing, right, left)):
        rsend[k] = attend(tile)
        share_out.append(go(remote(rsend.at[k], rrecv.at[x], rss.at[k], rsr.at[k], tile, y, z, c)))
        pump(4)
    rrecv[x] = attend(x)
    def wout_core(shard, sem):
        place = wout_s.at[shard, c]
        return remote(place, place, wxs.at[sem], wxr.at[sem], x, y, z, 1 - c)

    o_r1.wait_recv()
    o_cl = go(wout_core(left, 6))
    o_l0.wait_recv()
    o_cr = go(wout_core(right, 7))
    o_fr.wait_recv()
    o_fl.wait_recv()
    o_co = go(wout_core(facing, 8))
    pump(8)
    hid_s[...] = hall[:, :, pl.ds(pl.multiple_of(x * TILE, TILE), TILE)].reshape(D, TILE).astype(F32).T.astype(BF16)

    for k in range(9):
        rows = slice(k * 128, (k + 1) * 128)
        swap_s[rows, :] = (swap_column(k * 128, 128) == iota((128, D), 1).astype(F32)).astype(F32).astype(BF16)
    for copy in share_out:
        copy.wait_recv()
    o_cl.wait_recv()
    o_cr.wait_recv()
    o_co.wait_recv()
    attn_sum = dot_tn(rrecv[...].reshape(D, TILE), wout_s[...].reshape(D, D))
    residual = (hid_s[...].astype(F32) + rows_of(x, 2) * attn_sum).astype(BF16)
    resid_s[...] = residual
    values = normalized(residual.astype(F32))
    nmx[c] = (values * (1.0 + rows_of(x, 4)) + rows_of(x, 3)).astype(BF16)
    swap_mid = go(remote(nmx.at[c], nmx.at[c], exs.at[0], exr.at[0], x, y, z, 1 - c))
    pump(len(pending))
    row_steps = looked_up(row_lat == iota((64, 512), 1).astype(F32), lat_steps)
    row_hot = row_steps == iota((64, STEPS), 1).astype(F32)
    signal_now = looked_up(row_hot, now_ref[...])
    signal_next = looked_up(row_hot, next_ref[...])
    for copy in heads:
        copy.wait_recv()
    head = jnp.concatenate([nh_s[k].astype(F32) for k in range(4)], axis=1)
    head_rows = jnp.concatenate([head[0:8, :]] * 16 + [head[8:16, :]] * 16, axis=0).astype(BF16)

    swap_mid.wait_recv()
    both = nmx[...].reshape(256, D)
    both_swapped = dot(both, swap_s[...]).astype(BF16)

    def mlp(g, features):
        for key, copy in ring.items():
            if key[0] == g and key not in waited:
                copy.wait_recv()
        packed = w_all.at[g]
        expanded = dot(features, packed[:, :, 512:D].reshape(D, D - 512))[:, 64:64 + UNITS]
        activated = jax.nn.gelu(expanded, approximate=True).astype(BF16)
        return dot_nt(activated, packed[:, :, 0:UNITS].reshape(D, UNITS)).astype(BF16)

    mlp_part = mlp(0, both).astype(F32) + dot(mlp(1, both_swapped), swap_s[...])
    osend[...] = mlp_part.reshape(2, TILE, D)
    swap_out = go(remote(osend.at[1 - c], orecv, exs.at[1], exr.at[1], x, y, z, 1 - c))

    swap_out.wait_recv()
    mlp_sum = osend[c] + orecv[...]
    second = (resid_s[...].astype(F32) + rows_of(x, 5) * mlp_sum).astype(BF16)
    values = normalized(second.astype(F32))
    normed_out = (values * (1.0 + rows_of(x, 7)) + rows_of(x, 6)).astype(BF16)
    noise = dot_nt(normed_out, head_rows)
    token_col = iota((TILE, 256), 0) % GRIDW
    lane_col = (iota((TILE, 256), 1) % 128) // 8
    noise = jnp.where(token_col == lane_col, noise, 0.0)
    noise = jnp.sum(noise.reshape(8, GRIDW, 256), axis=1)
    nimg_w[pl.ds(0, 8, 2), :] = noise[:, 0:128]
    nimg_w[pl.ds(1, 8, 2), :] = noise[:, 128:256]
    nimg[x] = nimg_w[...]
    last = []
    for d in range(1, 4):
        tx = (x + d) % NX
        last.append(go(remote(nimg.at[x], nimg.at[x], fs.at[d], fr.at[d], tx, y, z, c)))
    for copy in last:
        copy.wait_recv()
    noise_img = nimg[...].reshape(64, 128)
    clean = (noisy_ref[...].astype(F32) - jnp.sqrt(1.0 - signal_now) * noise_img) / jnp.sqrt(signal_now)
    out_ref[0] = (
        jnp.sqrt(signal_next) * clean + jnp.sqrt(1.0 - signal_next) * noise_img).astype(BF16)
    blank = jnp.zeros((1, 128), F32)
    above = jnp.concatenate([blank, clean[:-1]], axis=0)
    below = jnp.concatenate([clean[1:], blank], axis=0)
    no_row = jnp.full((1, 1), -1.0, F32)
    above_ok = jnp.concatenate([no_row, row_lat[:-1]], axis=0) == row_lat
    below_ok = jnp.concatenate([row_lat[1:], no_row], axis=0) == row_lat
    preview = (
        jnp.where(above_ok, exact_dot(above, band_s[0]), 0.0)
        + exact_dot(clean, band_s[1])
        + jnp.where(below_ok, exact_dot(below, band_s[2]), 0.0)
    )
    out_ref[1] = preview.astype(BF16)

    for copy in sent:
        copy.wait_send()

    @pl.when(c != own_core)
    def _():
        line_weight(0, 0).wait_send()
        weight_x(from_left, block_l, 0, 80, 4, right).wait_send()
        weight_x(from_right, block_r, 80, 64, 5, left).wait_send()

    @pl.when(owner)
    def _():
        weight_x(is_b, block_id, 0, 80, 0, right).wait_send()
        weight_x(is_b, block_id, 80, 64, 2, left).wait_send()
        weight_x(is_b, block_id, 80, 64, 1, right).wait_send()
        weight_x(is_b, block_id, 0, 80, 3, left).wait_send()


def shards(
    hidden, noisy_latent, tile_latent, timesteps, step_embedding, alpha_now, alpha_next,
    modulation, attention_in, attention_out, expand_weight, reduce_weight, noise_head, preview_kernel,
):
    vmem = pl.BlockSpec(memory_space=pltpu.VMEM)
    dma = pltpu.SemaphoreType.DMA
    out = pl.pallas_call(
        kernel,
        out_shape=jax.ShapeDtypeStruct((2, 64, 128), BF16),
        in_specs=[vmem] * 7 + [pl.BlockSpec(memory_space=pl.ANY)] * 2 + [vmem] * 5,
        out_specs=vmem,
        scratch_shapes=[
            pltpu.VMEM((8, 16, COLS), BF16),
            pltpu.VMEM((16, 768), BF16),
            pltpu.VMEM((8, 16, COLS), BF16),
            pltpu.VMEM((8, 32, COLS), BF16),
            pltpu.VMEM((8, 32, COLS), BF16),
            pltpu.VMEM((8, 8, COLS), F32),
            pltpu.VMEM((8, 8, COLS), F32),
            pltpu.VMEM((2, 16, COLS), F32),
            pltpu.VMEM((4, 2, 16, COLS), F32),
            pltpu.VMEM((16, D), F32),
            pltpu.VMEM((4, 16, COLS), BF16),
            pltpu.VMEM((256, 128), BF16),
            pltpu.VMEM((4, COLS, 4 * TILE), BF16),
            pltpu.VMEM((D, 4 * TILE), F32),
            pltpu.VMEM((D, 4 * TILE), BF16),
            pltpu.VMEM((16, 16, 768), BF16),
            pltpu.VMEM((2, 8, BLOCK, D), BF16),
            pltpu.VMEM((3, COLS, D), BF16),
            pltpu.VMEM((4, 2, BLOCK, D), BF16),
            pltpu.VMEM((D, D), BF16),
            pltpu.VMEM((3 * COLS, 4 * TILE), BF16),
            pltpu.VMEM((HEADS_HERE, 4 * TILE, HEAD_DIM), BF16),
            pltpu.VMEM((COLS, TILE), F32),
            pltpu.VMEM((4, 1, 128), F32),
            pltpu.VMEM((3, COLS, TILE), BF16),
            pltpu.VMEM((4, COLS, TILE), BF16),
            pltpu.VMEM((TILE, D), BF16),
            pltpu.VMEM((TILE, D), BF16),
            pltpu.VMEM((2, TILE, D), BF16),
            pltpu.VMEM((2, TILE, D), F32),
            pltpu.VMEM((TILE, D), F32),
            pltpu.VMEM((4, 16, 128), F32),
            pltpu.VMEM((16, 128), F32),
            pltpu.VMEM((3, 128, 128), F32),
            dma((8,)), dma((8,)),
            dma((8,)), dma((8,)),
            dma((8,)), dma((8,)),
            dma((8,)), dma((8,)),
            dma((4,)), dma((4,)),
            dma((2,)),
            dma((6,)), dma((6,)),
            dma((8,)), dma((16,)),
            dma((6,)), dma((6,)),
            dma((64,)), dma((64,)),
            dma((9,)), dma((9,)),
            dma((3,)), dma((3,)),
            dma((2,)), dma((2,)),
            dma((4,)), dma((4,)),
        ],
        compiler_params=pltpu.CompilerParams(
            collective_id=0, has_side_effects=True, vmem_limit_bytes=60 * 1024 * 1024),
        name="dit_block",
    )(
        hidden.T, modulation, reduce_weight.T, expand_weight, step_embedding,
        tile_latent[None, :], timesteps[None, :], attention_in.transpose(1, 2, 0), attention_out.reshape(2, BLOCK, D),
        noise_head.T, noisy_latent, alpha_now[None, :], alpha_next[None, :], preview_kernel,
    )
    return (out[0], out[1])


def solution(mesh):
    return jax.shard_map(
        shards,
        mesh=mesh,
        in_specs=(
            P("row", "col"),
            P("row", None),
            P(),
            P(),
            P(),
            P(),
            P(),
            P("row", None, "col"),
            P(None, None, "col"),
            P("col", None),
            P("row", "col"),
            P("col", "row"),
            P("col", None),
            P(),
        ),
        out_specs=(P("row", None), P("row", None)),
        check_vma=False,
    )
```
